1024 devices in a mesh: comp: 8 (over x, core), tile: 128 (over z, y).
Axes of the slice: x: 4, y: 4, z: 32, core: 2. Of those that a mesh axis runs over, the one named last changes fastest.
Arguments:
- atmosphere_tracer_state: float32 [72, 32, 16384], P(None, 'comp', 'tile'), may hold values from -6 to 6
- courant: float32 [2, 72, 32, 16384], P(None, None, 'comp', 'tile'), may hold values from -0.24 to 0.24
- surface_exchange_factor: float32 [32, 16384], P('comp', 'tile'), may hold values from 0.3 to 3
- prior_sea_surface_temper: float32 [32, 16384], P('comp', 'tile'), may hold values from -6 to 6
- remap_overlay_weight: bfloat16 [8, 6144, 32, 128], P('comp', 'tile'), may hold values from 0.0029907227 to 0.099609375
- remap_dest_tile: int32 [8, 6144], P('comp', 'tile'), may hold values from 0 to 127, as said below
- remap_dest_block: int32 [8, 6144], P('comp', 'tile'), may hold values from 0 to 3
- ocean_level_state: float32 [2, 62, 32, 16384], P(None, None, 'comp', 'tile'), may hold values from -6 to 6
- ocean_cell_mask: int32 [32, 16384], P('comp', 'tile'), may hold values 0 or 1
Outputs:
- air_new: float32 [72, 32, 16384], P(None, 'comp', 'tile')
- ocean_new: float32 [2, 62, 32, 16384], P(None, None, 'comp', 'tile')
- surface_air: float32 [2, 32, 16384], P(None, 'comp', 'tile')
The draws below stay inside these ranges and needn't reach their ends.
Inputs may be any that keep to these rules, and one draw needn't show every extreme that they name: `remap_dest_tile`: among the 48 entries of one device, no ocean tile is named more than 2 times, and some tile is named exactly 2 times.
All inputs are finite; a program needn't handle non-finite values. No bound on the sum of `ocean_cell_mask` on one device may be relied on, other than what follows from the above.
Results may differ from the reference program's by a relative error of at most 0.0029.
Values may be sent and summed in bfloat16 or wider, within the bound.
No kernel may reach another device: no remote copies, remote signals or barrier semaphores. Data moves between devices by JAX's collectives and lax.ppermute only.
A program may use at most 32 MiB of HBM per device.

```python
import math
import jax
import jax.numpy as jnp
from jax import lax

AIR_LEVELS = 72
OLEV = 62
COLS = 128
AROWS = 4
OROWS = 4
ASUB = 32
OVL = 3
NSTEP = 4
NOSTEP = 2
ABLK = 16
ENT = 48
CAP = 2
NENT = 6144
AIR_GRID_ROWS = 32
NOR = 32
GRID_COLUMNS = 16384
N_COMP = 8
N_TILE = 128


def draw_remap_dest_tile(key, part):
    total = N_TILE * CAP

    def one_device(device_key):
        first_key, second_key = jax.random.split(device_key)
        full_tile = jax.random.randint(first_key, (), 0, N_TILE)
        shuffled = jax.random.permutation(second_key, total).astype(jnp.int32)
        slot_ids = jnp.arange(total, dtype=jnp.int32)
        order_key = shuffled + total * (slot_ids // CAP != full_tile).astype(jnp.int32)
        ordering = jnp.argsort(order_key).astype(jnp.int32)
        return (ordering[:ENT] // CAP).astype(jnp.int32)
    device_keys = jax.vmap(lambda index: jax.random.fold_in(key, index))(jnp.arange(N_COMP * N_TILE))
    return jax.vmap(one_device)(device_keys).reshape(N_COMP, N_TILE * ENT)


def touch_ends(values, rng, low, top_value):
    longest = values.shape.index(max(values.shape))
    spots = []
    for shift in (0, 1):
        where = [jax.random.randint(jax.random.fold_in(rng, axis), (), 0, length) for axis, length in enumerate(values.shape)]
        where[longest] = (where[longest] + shift) % values.shape[longest]
        spots.append(tuple(where))
    return values.at[spots[0]].set(low).at[spots[1]].set(top_value)


def block_levels(rng, extent, cuts, low, largest):
    def one(position, blocks):
        draws = jax.random.uniform(jax.random.fold_in(jax.random.fold_in(rng, 6), position), (blocks,), jnp.float32, low / len(cuts), largest / len(cuts))
        return jnp.repeat(jnp.exp(draws), extent[position] // blocks).reshape((-1,) + (1,) * (len(extent) - position - 1))

    factor_of = one(*cuts[0])
    for cut in cuts[1:]:
        factor_of = factor_of * one(*cut)
    return factor_of


def scatter_about(stream_key, shape, scale, bound, pieces=(), kind=jnp.bfloat16):
    values = jax.random.normal(stream_key, shape, jnp.float32) * scale
    if len(pieces) > 0:
        values = block_levels(stream_key, shape, pieces, -0.22, 0.18) * values
    return jnp.clip(values, min=-bound, max=bound).astype(kind)


def setup_inputs(seed: int = 0) -> dict:
    keys = jax.random.split(jax.random.key(seed), 10)
    return {
        "atmosphere_tracer_state": scatter_about(keys[0], (AIR_LEVELS, AIR_GRID_ROWS, GRID_COLUMNS), 1.0, 6.0, ((1, 8), (2, 128)), jnp.float32),
        "courant": jnp.clip(jax.random.uniform(keys[1], (2, AIR_LEVELS, AIR_GRID_ROWS, GRID_COLUMNS), jnp.float32, -0.24, 0.24) * block_levels(keys[1], (2, AIR_LEVELS, AIR_GRID_ROWS, GRID_COLUMNS), ((2, 8), (3, 128)), -0.4, 0.0), -0.24, 0.24),
        "surface_exchange_factor": jnp.clip(jnp.exp(math.log(3.0) - 2.3025851 * jax.random.uniform(keys[2], (AIR_GRID_ROWS, GRID_COLUMNS), jnp.float32) ** block_levels(keys[2], (AIR_GRID_ROWS, GRID_COLUMNS), ((0, 8), (1, 128)), -0.2, 0.2)), 0.3, 3.0),
        "prior_sea_surface_temper": scatter_about(keys[3], (AIR_GRID_ROWS, GRID_COLUMNS), 1.0, 6.0, ((0, 8), (1, 128)), jnp.float32),
        "remap_overlay_weight": jnp.clip(jnp.exp(math.log(0.099609375) - 3.5057412 * jax.random.uniform(keys[4], (N_COMP, NENT, ASUB, COLS), jnp.float32) ** block_levels(keys[4], (N_COMP, NENT, ASUB, COLS), ((0, 8), (1, 128)), -0.2, 0.2)), 0.0029907227, 0.099609375).astype(jnp.bfloat16),
        "remap_dest_tile": draw_remap_dest_tile(jax.random.fold_in(keys[9], 71), 0),
        "remap_dest_block": touch_ends(jax.random.randint(keys[6], (N_COMP, NENT), 0, OROWS), jax.random.fold_in(keys[6], 1), 0, OROWS - 1).astype(jnp.int32),
        "ocean_level_state": scatter_about(keys[7], (2, OLEV, NOR, GRID_COLUMNS), 1.0, 6.0, ((2, 8), (3, 128)), jnp.float32),
        "ocean_cell_mask": touch_ends((jax.random.randint(keys[8], (NOR, GRID_COLUMNS), 0, 4) < 3).astype(jnp.int32), jax.random.fold_in(keys[8], 1), 0, 1),
    }


hor_mix = 0.12
vert_mix = 0.2
press_grad = 0.3


def air_step(tracer_field, courant):
    east_cour = courant[0]
    north_cour = courant[1]
    east_flux = jnp.maximum(east_cour, 0.0) * tracer_field + jnp.minimum(east_cour, 0.0) * jnp.roll(tracer_field, -1, axis=2)
    north_flux = jnp.maximum(north_cour, 0.0) * tracer_field + jnp.minimum(north_cour, 0.0) * jnp.roll(tracer_field, -1, axis=1)
    return tracer_field - (east_flux - jnp.roll(east_flux, 1, axis=2)) - (north_flux - jnp.roll(north_flux, 1, axis=1))


def sea_step(state, force, wet):
    laplace = jnp.roll(state, 1, 2) + jnp.roll(state, -1, 2) + jnp.roll(state, 1, 3) + jnp.roll(state, -1, 3) - 4.0 * state
    diffs = state[:, 1:] - state[:, :-1]
    zeros_lev = jnp.zeros_like(state[:, :1])
    vertical = jnp.concatenate([diffs, zeros_lev], axis=1) - jnp.concatenate([zeros_lev, diffs], axis=1)
    temper = state[0]
    gradient = jnp.roll(temper, -1, axis=2) - jnp.roll(temper, 1, axis=2)
    tend_temp = hor_mix * laplace[0] + vert_mix * vertical[0]
    tend_temp = tend_temp.at[0].add(force)
    tend_cur = hor_mix * laplace[1] + vert_mix * vertical[1] - press_grad * gradient
    return state + wet * jnp.stack([tend_temp, tend_cur])


def reference(atmosphere_tracer_state, courant, surface_exchange_factor, prior_sea_surface_temper, remap_overlay_weight, remap_dest_tile, remap_dest_block, ocean_level_state, ocean_cell_mask):
    tracer_field = atmosphere_tracer_state
    for sweep_index in range(NSTEP):
        tracer_field = air_step(tracer_field, courant)
    transport_flux = (surface_exchange_factor * (tracer_field[AIR_LEVELS - 1] - prior_sea_surface_temper)).astype(jnp.bfloat16)
    subs = COLS // ASUB
    flux_blocks = transport_flux.reshape(N_COMP, AROWS, N_TILE, subs, ASUB).transpose(0, 2, 1, 3, 4)
    flux_blocks = flux_blocks.reshape(N_COMP, N_TILE, ABLK, ASUB)
    flux_blocks = jnp.repeat(flux_blocks, OVL, axis=2).reshape(N_COMP, NENT, ASUB)

    def remap_band(pair):
        weight_band, flux_band = pair
        prod = jnp.einsum('nk,nko->no', flux_band.astype(jnp.float32), weight_band.astype(jnp.float32), precision=lax.Precision.HIGHEST)
        return prod.astype(jnp.bfloat16)

    contrib = lax.map(remap_band, (remap_overlay_weight, flux_blocks))
    band_ids = jnp.arange(N_COMP, dtype=jnp.int32)[:, None]
    target = band_ids * (N_TILE * OROWS) + remap_dest_tile * OROWS + remap_dest_block
    force = jax.ops.segment_sum(contrib.astype(jnp.float32).reshape(-1, COLS), target.reshape(-1), num_segments=N_COMP * N_TILE * OROWS)
    force = force.reshape(N_COMP, N_TILE, OROWS, COLS).transpose(0, 2, 1, 3).reshape(NOR, GRID_COLUMNS)
    wet = ocean_cell_mask.astype(jnp.float32)
    state = ocean_level_state
    for sweep_index in range(NOSTEP):
        state = sea_step(state, force, wet)
    surface = state[:, 0].astype(jnp.bfloat16)
    grid = surface.reshape(2, N_COMP, OROWS, N_TILE, COLS)
    values = grid[:, band_ids, remap_dest_block, remap_dest_tile, :]
    values = values.transpose(1, 2, 0, 3)

    def back_band(pair):
        weight_band, value_band = pair
        weight_full = weight_band.astype(jnp.float32)
        summed = jnp.einsum('nko,nco->nck', weight_full, value_band.astype(jnp.float32), precision=lax.Precision.HIGHEST)
        areas = jnp.sum(weight_full, axis=2)
        summed = summed.reshape(N_TILE, ABLK, OVL, 2, ASUB).sum(axis=2)
        areas = areas.reshape(N_TILE, ABLK, OVL, ASUB).sum(axis=2)
        return summed / areas[:, :, None, :]

    ratio = lax.map(back_band, (remap_overlay_weight, values))
    ratio = ratio.reshape(N_COMP, N_TILE, AROWS, subs, 2, ASUB).transpose(4, 0, 2, 1, 3, 5)
    surface_air = ratio.reshape(2, AIR_GRID_ROWS, GRID_COLUMNS)
    return tracer_field, state, surface_air
```

```python
import jax
import jax.numpy as jnp
from jax import lax
from jax.sharding import PartitionSpec as P

OVL = 3
NSTEP = 4
NOSTEP = 2
EDGE = 4

hor_mix = 0.12
vert_mix = 0.2
press_grad = 0.3


bf16 = jnp.bfloat16
f32 = jnp.float32


def dot(a, b, ca, cb):
    return lax.dot_general(a, b, (((ca,), (cb,)), ((), ())), preferred_element_type=f32)


def ring(axis, step):
    size = lax.axis_size(axis)
    return [(i, (i + step) % size) for i in range(size)]


def air_steps(q, cx, cy):
    for _ in range(NSTEP):
        n = q.shape[0]
        lo = (cx.shape[0] - n) // 2
        ex, ny = cx[lo + 1 : lo + n - 1], cy[lo : lo + n - 1]
        mid = q[1:-1]
        east = jnp.maximum(ex, 0.0) * mid + jnp.minimum(ex, 0.0) * jnp.roll(mid, -1, -1)
        north = jnp.maximum(ny, 0.0) * q[:-1] + jnp.minimum(ny, 0.0) * q[1:]
        q = mid - (east - jnp.roll(east, 1, -1)) - (north[1:] - north[:-1])
    return q


def sea_steps(state, wet):
    for _ in range(NOSTEP):
        n = state.shape[1]
        lo = (wet.shape[0] - (n - 2)) // 2
        w = wet[lo : lo + n - 2][:, None, :]
        mid = state[:, 1:-1]
        ahead, behind = jnp.roll(mid, -1, -1), jnp.roll(mid, 1, -1)
        laplace = state[:, 2:] + state[:, :-2] + ahead + behind - 4.0 * mid
        diffs = mid[:, :, 1:] - mid[:, :, :-1]
        zeros = jnp.zeros_like(mid[:, :, :1])
        vertical = jnp.concatenate([diffs, zeros], 2) - jnp.concatenate([zeros, diffs], 2)
        tend = hor_mix * laplace + vert_mix * vertical
        gradient = ahead[0] - behind[0]
        tend = jnp.stack([tend[0], tend[1] - press_grad * gradient])
        state = mid + w * tend
    return state


def body(
    atmosphere_tracer_state,
    courant,
    surface_exchange_factor,
    prior_sea_surface_temper,
    remap_overlay_weight,
    remap_dest_tile,
    remap_dest_block,
    ocean_level_state,
    ocean_cell_mask,
):
    levels, rows, cols = atmosphere_tracer_state.shape
    olev = ocean_level_state.shape[1]
    weights = remap_overlay_weight[0]
    tiles = remap_dest_tile[0]
    blocks = remap_dest_block[0]
    entries, sub, _ = weights.shape
    ntile = lax.axis_size("tile")
    i32 = jnp.int32

    ent = jnp.arange(entries, dtype=i32)
    rank = jnp.sum(((tiles[:, None] == tiles[None, :]) & (ent[None, :] < ent[:, None])).astype(i32), axis=1)
    orow = jnp.arange(4 * ntile, dtype=i32)[:, None]
    otile, oslot = orow // 4, orow % 4
    t, k = tiles[None, :], rank[None, :]
    own = ((otile == t) & (oslot == k)).astype(bf16)
    aux_row = oslot == 2
    west_of = (t + 1 == otile) | ((t == ntile - 1) & (otile == 0))
    east_of = (t - 1 == otile) | ((t == 0) & (otile == ntile - 1))
    spread = jnp.concatenate(
        [own, (aux_row & (otile == t)).astype(bf16), (aux_row & west_of).astype(bf16), (aux_row & east_of).astype(bf16)], axis=1
    )
    lane = jnp.arange(cols, dtype=i32)[None, :]
    hit = (lane % 4 == blocks[:, None]) & ((lane // 4) % 2 == rank[:, None])
    label = (hit & (lane < 16)).astype(bf16)
    west_hit = hit & (lane >= 16) & (lane < 24)
    east_hit = hit & (lane >= 24) & (lane < 32)

    air32 = jnp.concatenate([atmosphere_tracer_state[None], courant], axis=0).transpose(0, 2, 1, 3)
    air = air32.astype(bf16)
    sea32 = ocean_level_state.transpose(0, 2, 1, 3)
    sea = sea32.astype(bf16)
    wet16 = ocean_cell_mask.astype(bf16)
    n_air, n_sea = 3 * rows * levels, 2 * 2 * olev

    def pack(part, wet_row):
        return jnp.concatenate([air.reshape(-1, cols), part.reshape(-1, cols), wet_row], axis=0)

    def unpack(got):
        return (
            got[:n_air].reshape(3, rows, levels, cols),
            got[n_air : n_air + n_sea].reshape(2, 2, olev, cols),
            got[n_air + n_sea :],
        )

    before = unpack(lax.ppermute(pack(sea[:, rows - 2 :], wet16[rows - 1 :]), "comp", ring("comp", 1)))
    after = unpack(lax.ppermute(pack(sea[:, :2], wet16[:1]), "comp", ring("comp", -1)))
    tall_air = jnp.concatenate([before[0], air, after[0]], axis=1)
    tall_sea = jnp.concatenate([before[1], sea, after[1]], axis=1)
    tall_wet = jnp.concatenate([before[2], wet16, after[2]], axis=0)
    arow, srow = 3 * rows, rows + 4
    stack = jnp.concatenate(
        [
            tall_air.reshape(-1, cols),
            jnp.pad(tall_sea, ((0, 0), (0, 0), (0, 64 - olev), (0, 0))).reshape(-1, cols),
            jnp.pad(tall_wet, ((0, 8 - rows - 2), (0, 0))),
        ],
        axis=0,
    )
    edge = jnp.arange(2 * EDGE, dtype=i32)[:, None]
    place = (lane == edge + jnp.where(edge < EDGE, 0, cols - 2 * EDGE)).astype(bf16)
    strips = dot(place, stack, 1, 1).astype(bf16)
    from_east = lax.ppermute(strips[:EDGE], "tile", ring("tile", -1))
    from_west = lax.ppermute(strips[EDGE:], "tile", ring("tile", 1))
    beyond = dot(jnp.concatenate([from_east, from_west], axis=0), place, 0, 0)
    n_tall = 3 * arow * levels
    far_air = beyond[:n_tall].reshape(3, arow, levels, cols)
    far_sea = beyond[n_tall : n_tall + 2 * srow * 64].reshape(2, srow, 64, cols)[:, :, :olev]
    far_wet = beyond[n_tall + 2 * srow * 64 :][: rows + 2]

    def wide(mid, low, high, far, axis):
        main = jnp.concatenate([low.astype(f32), mid, high.astype(f32)], axis=axis)
        return jnp.concatenate([main, far], axis=-1)

    last = levels - 1
    low_air = wide(air32[:, :, last], before[0][:, :, last], after[0][:, :, last], far_air[:, :, last], 1)
    bottom = air_steps(low_air[0], low_air[1], low_air[2])[:, :cols]
    flux = (surface_exchange_factor * (bottom - prior_sea_surface_temper)).astype(bf16)
    flux_blocks = jnp.repeat(flux.reshape(-1, sub), OVL, axis=0)
    contrib = jnp.einsum("ek,eko->eo", flux_blocks, weights, preferred_element_type=f32).astype(bf16)
    zero = jnp.zeros((), bf16)
    west_cells = jnp.where(west_hit, contrib[:, cols - 1 :], zero)
    east_cells = jnp.where(east_hit, contrib[:, :1], zero)
    outgoing = dot(spread, jnp.concatenate([contrib, label, west_cells, east_cells], axis=0), 1, 0).astype(bf16)
    arrived = lax.all_to_all(outgoing.reshape(ntile, 4, cols), "tile", split_axis=0, concat_axis=0, tiled=True)
    arrived = arrived.reshape(4 * ntile, cols)

    col_id = jnp.arange(4 * ntile, dtype=i32)[None, :]
    aux_of = (col_id == (orow // 4) * 4 + 2).astype(bf16)
    aux = dot(aux_of, arrived, 1, 0).astype(bf16)
    picks = jnp.where((lane < 8) & (lane // 4 == oslot), aux, zero)
    gathered = dot(picks, arrived, 0, 0)
    force = gathered[:rows] + gathered[rows : 2 * rows]
    is_aux = jnp.broadcast_to(col_id % 4 == 2, (8, 4 * ntile)).astype(bf16)
    sums = dot(is_aux, arrived, 1, 0)[0]
    west_force = sums[16:20] + sums[20:24]
    east_force = sums[24:28] + sums[28:32]
    wet = ocean_cell_mask.astype(f32)
    pushed = wet * force
    west_pushed = far_wet[1:-1, cols - 1 :] * west_force[:, None]
    east_pushed = far_wet[1:-1, :1] * east_force[:, None]
    below = lax.ppermute(pushed[rows - 1 :], "comp", ring("comp", 1))
    above = lax.ppermute(pushed[:1], "comp", ring("comp", -1))
    returns = jnp.where((lane < 16) & (lane // 4 == (oslot % 2) * 2 + oslot // 2), aux, zero)

    wide_sea = wide(sea32, before[1], after[1], far_sea, 1)
    wide_wet = jnp.concatenate([tall_wet.astype(f32), far_wet], axis=-1)
    base = sea_steps(wide_sea, wide_wet)[..., :cols]
    ahead = jnp.concatenate([pushed[:, 1:], east_pushed], axis=1)
    behind = jnp.concatenate([west_pushed, pushed[:, :-1]], axis=1)
    upper = jnp.concatenate([pushed[1:], above], axis=0)
    lower = jnp.concatenate([below, pushed[:-1]], axis=0)
    lap = upper + lower + ahead + behind - 4.0 * pushed
    temp0 = base[0, :, 0] + (2.0 * pushed + wet * (hor_mix * lap - vert_mix * pushed))
    temp1 = base[0, :, 1] + wet * (vert_mix * pushed)
    cur0 = base[1, :, 0] - wet * (press_grad * (ahead - behind))
    surface = jnp.stack([temp0, cur0]).astype(bf16)

    s2 = jnp.concatenate([surface[0], surface[0], surface[1], surface[1]], axis=0)
    sent = dot(returns[:, :16], s2, 1, 0).astype(bf16)
    came = lax.all_to_all(sent.reshape(ntile, 4, cols), "tile", split_axis=0, concat_axis=0, tiled=True)
    came = came.reshape(4 * ntile, cols)
    at = tiles * 4 + rank * 2
    want = (jnp.stack([at, at + 1], axis=1).reshape(-1)[:, None] == col_id).astype(bf16)
    values = dot(want, came, 1, 0).astype(bf16).reshape(entries, 2, cols)
    summed = jnp.einsum("eko,eco->eck", weights, values, preferred_element_type=f32)
    areas = jnp.sum(weights.astype(f32), axis=2)
    count = entries // OVL
    summed = summed.reshape(count, OVL, 2, sub).sum(axis=1)
    areas = areas.reshape(count, OVL, sub).sum(axis=1)
    ratio = summed / areas[:, None, :]
    ratio = ratio.reshape(rows, cols // sub, 2, sub).transpose(2, 0, 1, 3)
    surface_air = ratio.reshape(2, rows, cols)

    wide_air = wide(air32, before[0], after[0], far_air, 1)
    air_new = air_steps(wide_air[0], wide_air[1], wide_air[2])[..., :cols].transpose(1, 0, 2)
    temp = jnp.concatenate([temp0[:, None], temp1[:, None], base[0, :, 2:]], axis=1)
    cur = jnp.concatenate([cur0[:, None], base[1, :, 1:]], axis=1)
    ocean_new = jnp.stack([temp, cur]).transpose(0, 2, 1, 3)
    return (air_new, ocean_new, surface_air)


def solution(mesh):
    return jax.shard_map(
        body,
        mesh=mesh,
        in_specs=(
            P(None, "comp", "tile"),
            P(None, None, "comp", "tile"),
            P("comp", "tile"),
            P("comp", "tile"),
            P("comp", "tile", None, None),
            P("comp", "tile"),
            P("comp", "tile"),
            P(None, None, "comp", "tile"),
            P("comp", "tile"),
        ),
        out_specs=(P(None, "comp", "tile"), P(None, None, "comp", "tile"), P(None, "comp", "tile")),
        check_vma=False,
    )
```

```python
import functools

import jax
import jax.numpy as jnp
from jax import lax
from jax.experimental import pallas as pl
from jax.experimental.pallas import tpu as pltpu
from jax.sharding import PartitionSpec as P

OVL = 3
NSTEP = 4
NOSTEP = 2
INTERPRET = False

hor_mix = 0.12
vert_mix = 0.2
press_grad = 0.3


bf16 = jnp.bfloat16
f32 = jnp.float32
i32 = jnp.int32

LEV, OL, ROWS, COLS, SUB, ENTS = 72, 62, 4, 128, 32, 48
NAIR = 3 * LEV * ROWS
NA1 = LEV * ROWS
NSEA = OL * ROWS
OLP = 64
SEA0 = NAIR
WET0 = SEA0 + 4 * OLP
LOW0 = WET0 + 16
NMSG = LOW0 + 16
OSEA0 = NAIR
OWET0 = OSEA0 + 2 * NSEA
OLOW0 = OWET0 + 16
NOWN = OLOW0 + 32
NSTR = 2 * NMSG + NOWN
PADE = 64


def dot(a, b, ca, cb, **kw):
    return lax.dot_general(a, b, (((ca,), (cb,)), ((), ())), preferred_element_type=f32, **kw)


def iota(shape, axis):
    return lax.broadcasted_iota(i32, shape, axis)


def onehot(mask):
    return jnp.where(mask, 1.0, 0.0).astype(bf16)


def call(kernel, outs, *args, scratch=()):
    return pl.pallas_call(
        kernel,
        out_shape=outs,
        scratch_shapes=list(scratch),
        compiler_params=None if INTERPRET else pltpu.CompilerParams(vmem_limit_bytes=48 << 20),
        interpret=INTERPRET,
    )(*args)


def ring(axis, step):
    size = lax.axis_size(axis)
    return [(i, (i + step) % size) for i in range(size)]


def low_rows(q_ref, c_ref):
    pieces = [q_ref[NA1 - 4 : NA1, :], c_ref[NA1 - 4 : NA1, :], c_ref[2 * NA1 - 4 : 2 * NA1, :]]
    return jnp.concatenate(pieces + [jnp.zeros((4, COLS), f32)], axis=0).astype(bf16)


def pack_kernel(q_ref, c_ref, x_ref, m_ref, up_ref, down_ref):
    q = q_ref[...].astype(bf16)
    c = c_ref[...].astype(bf16)
    low = low_rows(q_ref, c_ref)
    mask = m_ref[...].astype(f32)
    for ref, r0, mr in ((up_ref, ROWS - 2, ROWS - 1), (down_ref, 0, 0)):
        ref[0:NA1, :] = q
        ref[NA1:NAIR, :] = c
        for v in range(2):
            for r in range(2):
                at = SEA0 + (2 * v + r) * OLP
                part = x_ref[pl.ds(v * NSEA + r0 + r, OL, stride=ROWS), :]
                ref[at : at + OLP, :] = jnp.concatenate([part, jnp.zeros((OLP - OL, COLS), f32)], axis=0).astype(bf16)
        ref[WET0:LOW0, :] = jnp.broadcast_to(mask[mr : mr + 1], (16, COLS)).astype(bf16)
        ref[LOW0:NMSG, :] = low


def place_matrix(first):
    j, lane = iota((8, COLS), 0), iota((8, COLS), 1)
    return onehot((j < 4) & (lane == (j if first else j + COLS - 4)))


def strip_kernel(q_ref, c_ref, x_ref, m_ref, b_ref, a_ref, west_ref, east_ref):
    mask = jnp.concatenate([m_ref[...].astype(f32), jnp.zeros((12, COLS), f32)], axis=0).astype(bf16)
    tail = jnp.concatenate([mask, low_rows(q_ref, c_ref), jnp.zeros((16, COLS), bf16)], axis=0)
    own = jnp.concatenate([q_ref[...].astype(bf16), c_ref[...].astype(bf16), x_ref[...].astype(bf16), tail], axis=0)
    for ref, first in ((west_ref, True), (east_ref, False)):
        place = place_matrix(first)
        ref[:, 0:NMSG] = dot(place, b_ref[...], 1, 1).astype(bf16)
        ref[:, NMSG : NMSG + NOWN] = dot(place, own, 1, 1).astype(bf16)
        ref[:, NMSG + NOWN :] = dot(place, a_ref[...], 1, 1).astype(bf16)


def beyond(fe, fw):
    both = fe.astype(f32) + pltpu.roll(fw.astype(f32), 4, 0)
    j, lane = iota((8, COLS), 0), iota((8, COLS), 1)
    place = jnp.where(lane == jnp.where(j < 4, j, j + COLS - 8), 1.0, 0.0)
    return dot(both, place, 0, 0)


def entry_tables(tc_ref, tr_ref):
    tcol = tc_ref[...]
    trow = tr_ref[...]
    e, l = iota((PADE, 4 * PADE), 0), iota((PADE, 4 * PADE), 1)
    same = tcol == trow
    rank_row = jnp.sum(jnp.where(same & (e < l % PADE), 1, 0), axis=0, keepdims=True)
    rank_col = jnp.sum(jnp.where(same & (l < e), 1, 0), axis=1, keepdims=True)
    return tcol, trow, rank_col, rank_row


def flux_kernel(ntile, q_ref, c_ref, b_ref, a_ref, fe_ref, fw_ref, f_ref, p_ref, w_ref, tc_ref, tr_ref, bc_ref, out_ref):
    parts = []
    mine = (q_ref[NA1 - 4 : NA1, :], c_ref[NA1 - 4 : NA1, :], c_ref[2 * NA1 - 4 : 2 * NA1, :])
    nb = b_ref[LOW0:NMSG, :].astype(f32)
    na = a_ref[LOW0:NMSG, :].astype(f32)
    lo_b = beyond(fe_ref[:, NMSG - COLS : NMSG], fw_ref[:, NMSG - COLS : NMSG])[COLS - 16 :]
    o1 = NMSG + NOWN
    lo_o = beyond(fe_ref[:, o1 - COLS : o1], fw_ref[:, o1 - COLS : o1])[COLS - 32 : COLS - 16]
    lo_a = beyond(fe_ref[:, NSTR - COLS :], fw_ref[:, NSTR - COLS :])[COLS - 16 :]
    pad = jnp.zeros((4, COLS), f32)
    for i in range(3):
        s = slice(4 * i, 4 * i + 4)
        main = jnp.concatenate([nb[s], mine[i], na[s], pad], axis=0)
        far = jnp.concatenate([lo_b[s], lo_o[s], lo_a[s], pad], axis=0)
        parts.append(jnp.concatenate([main, far], axis=1))
    q, cx, cy = parts
    xp, xm, yp, ym = jnp.maximum(cx, 0.0), jnp.minimum(cx, 0.0), jnp.maximum(cy, 0.0), jnp.minimum(cy, 0.0)
    for _ in range(NSTEP):
        east = xp * q + xm * pltpu.roll(q, 2 * COLS - 1, 1)
        north = yp * q + ym * pltpu.roll(q, 15, 0)
        q = q - (east - pltpu.roll(east, 1, 1)) - (north - pltpu.roll(north, 1, 0))
    flux = f_ref[...] * (q[ROWS : 2 * ROWS, :COLS] - p_ref[...])
    flux = jnp.concatenate([flux, jnp.zeros((4, COLS), f32)], axis=0).astype(bf16).astype(f32)
    turned = jnp.concatenate([flux] + [pltpu.roll(flux, SUB * d, 1) for d in range(1, 4)], axis=0).astype(bf16)
    e, k = iota((PADE, 32), 0), iota((PADE, 32), 1)
    turn = (e % 4 - (e // 3) % 4 + 4) % 4
    pick = onehot((e < ENTS) & (k == turn * 8 + e // 12))
    lined = dot(pick, turned, 1, 0)
    e, lane = iota((PADE, COLS), 0), iota((PADE, COLS), 1)
    lined = jnp.where(lane // SUB == e % 4, lined, 0.0)
    spread_flux = jnp.concatenate([jnp.where(e // 4 == j, lined, 0.0) for j in range(ENTS // 4)], axis=1).astype(bf16)
    contrib = dot(spread_flux, w_ref[...], 1, 0).astype(bf16).astype(f32)
    tcol, trow, rank_col, rank_row = entry_tables(tc_ref, tr_ref)
    hit = (lane % 4 == bc_ref[...]) & ((lane // 4) % 2 == rank_col)
    label = jnp.where(hit & (lane < 16), 1.0, 0.0)
    west = jnp.where(hit & (lane >= 16) & (lane < 24), contrib[:, COLS - 1 :], 0.0)
    east = jnp.where(hit & (lane >= 24) & (lane < 32), contrib[:, :1], 0.0)
    table = jnp.concatenate([contrib, label, west, east], axis=0).astype(bf16)
    kind = iota((1, 4 * PADE), 1) // PADE
    to = jnp.where(kind == 2, jnp.where(trow == ntile - 1, 0, trow + 1), trow)
    to = jnp.where(kind == 3, jnp.where(trow == 0, ntile - 1, trow - 1), to)
    slot = jnp.where(kind == 0, rank_row, 2)
    where_to = to * 4 + slot
    spread = onehot(iota((4 * ntile, 4 * PADE), 0) == where_to)
    out_ref[...] = dot(spread, table, 1, 0).astype(bf16)


def sea_kernel(x_ref, m_ref, b_ref, a_ref, fe_ref, fw_ref, out_ref, wide_ref, x_s, fb_s, fo_s, fa_s):
    o0, o1 = NMSG, NMSG + NOWN
    fb_s[...] = beyond(fe_ref[:, 0:o0], fw_ref[:, 0:o0])
    fo_s[...] = beyond(fe_ref[:, o0:o1], fw_ref[:, o0:o1])
    fa_s[...] = beyond(fe_ref[:, o1:], fw_ref[:, o1:])
    x_s[0 : 2 * NSEA, :] = x_ref[...]
    x_s[2 * NSEA :, :] = jnp.zeros((16, COLS), f32)

    def join(main, far):
        return jnp.concatenate([main, far], axis=1)

    wet = [join(b_ref[WET0 : WET0 + 16, :].astype(f32)[:1], fb_s[WET0 : WET0 + 1, :])]
    mask = m_ref[...].astype(f32)
    for r in range(ROWS):
        wet.append(join(mask[r : r + 1], fo_s[OWET0 + r : OWET0 + r + 1, :]))
    wet.append(join(a_ref[WET0 : WET0 + 16, :].astype(f32)[:1], fa_s[WET0 : WET0 + 1, :]))
    wide_ref[...] = jnp.concatenate(wet + [jnp.zeros((2, 2 * COLS), f32)], axis=0)
    level = iota((OLP, 2 * COLS), 0)
    top, bottom = level == 0, level >= OL - 1

    state = []
    for v in range(2):
        rows = []
        for r in range(2):
            at = SEA0 + (2 * v + r) * OLP
            rows.append(join(b_ref[at : at + OLP, :].astype(f32), fb_s[at : at + OLP, :]))
        for r in range(ROWS):
            at = v * NSEA + r
            rows.append(join(x_s[pl.ds(at, OLP, stride=ROWS), :], fo_s[pl.ds(OSEA0 + at, OLP, stride=ROWS), :]))
        for r in range(2):
            at = SEA0 + (2 * v + r) * OLP
            rows.append(join(a_ref[at : at + OLP, :].astype(f32), fa_s[at : at + OLP, :]))
        state.append(rows)
    for step in range(NOSTEP):
        new = [[], []]
        for j in range(1, len(state[0]) - 1):
            w = wet[j - 1 + step]
            for v in range(2):
                mid = state[v][j]
                ahead, behind = pltpu.roll(mid, 2 * COLS - 1, 1), pltpu.roll(mid, 1, 1)
                lap = state[v][j + 1] + state[v][j - 1] + ahead + behind - 4.0 * mid
                under = jnp.where(bottom, 0.0, pltpu.roll(mid, OLP - 1, 0) - mid)
                over = jnp.where(top, 0.0, mid - pltpu.roll(mid, 1, 0))
                tend = hor_mix * lap + vert_mix * (under - over)
                if v == 0:
                    gradient = ahead - behind
                else:
                    tend = tend - press_grad * gradient
                new[v].append(mid + w * tend)
        state = new
    for v in range(2):
        for r in range(ROWS):
            out_ref[pl.ds(v * NSEA + r, OL, stride=ROWS), :] = state[v][r][:OL, :COLS]


def force_kernel(ntile, got_ref, wide_ref, aux_ref, keep_ref, up_ref, down_ref, s_ref):
    s_ref[...] = got_ref[...].astype(f32)
    first = s_ref[pl.ds(0, ntile, stride=4), :].astype(bf16)
    second = s_ref[pl.ds(1, ntile, stride=4), :].astype(bf16)
    aux32 = s_ref[pl.ds(2, ntile, stride=4), :]
    aux = aux32.astype(bf16)
    aux_ref[...] = aux
    force = dot(aux32, first.astype(f32), 0, 0)[0:4] + dot(aux32, second.astype(f32), 0, 0)[4:8]
    sums = jnp.sum(aux32, axis=0, keepdims=True)
    r, lane = iota((ROWS, COLS), 0), iota((ROWS, COLS), 1)
    mine = lane % 4 == r
    west = jnp.sum(jnp.where(mine & (lane >= 16) & (lane < 24), sums, 0.0), axis=1, keepdims=True)
    east = jnp.sum(jnp.where(mine & (lane >= 24) & (lane < 32), sums, 0.0), axis=1, keepdims=True)
    wet = wide_ref[1 : ROWS + 1, :]
    pushed = wet[:, :COLS] * force
    west = wet[:, 2 * COLS - 1 :] * west
    east = wet[:, COLS : COLS + 1] * east
    ahead = jnp.where(lane == COLS - 1, east, pltpu.roll(jnp.concatenate([pushed, pushed], axis=0), COLS - 1, 1)[:ROWS])
    behind = jnp.where(lane == 0, west, pltpu.roll(jnp.concatenate([pushed, pushed], axis=0), 1, 1)[:ROWS])
    keep_ref[...] = jnp.concatenate([pushed, ahead, behind, wet[:, :COLS]], axis=0)
    up_ref[...] = jnp.broadcast_to(pushed[ROWS - 1 :], (8, COLS))
    down_ref[...] = jnp.broadcast_to(pushed[:1], (8, COLS))


def surface_kernel(ntile, base_ref, keep_ref, below_ref, above_ref, aux_ref, sent_ref, top_ref, s_ref):
    pushed, ahead, behind = keep_ref[0:4, :], keep_ref[4:8, :], keep_ref[8:12, :]
    wet = keep_ref[12:16, :]
    upper = jnp.concatenate([pushed[1:], above_ref[0:1, :]], axis=0)
    lower = jnp.concatenate([below_ref[0:1, :], pushed[:-1]], axis=0)
    lap = upper + lower + ahead + behind - 4.0 * pushed
    temp0 = base_ref[0:4, :] + (2.0 * pushed + wet * (hor_mix * lap - vert_mix * pushed))
    temp1 = base_ref[4:8, :] + wet * (vert_mix * pushed)
    cur0 = base_ref[NSEA : NSEA + 4, :] - wet * (press_grad * (ahead - behind))
    top_ref[...] = jnp.concatenate([temp0, temp1, cur0, jnp.zeros((4, COLS), f32)], axis=0)
    table = jnp.concatenate([temp0, temp0, cur0, cur0], axis=0)
    row = iota((16, COLS), 0)
    aux = aux_ref[...][:, :16]
    for slot in range(2):
        for c in range(2):
            part = jnp.where(row // 4 == 2 * c + slot, table, 0.0).astype(bf16)
            s_ref[pl.ds(2 * slot + c, ntile, stride=4), :] = dot(aux, part, 1, 0)
    sent_ref[...] = s_ref[...].astype(bf16)


def air_kernel(q_ref, c_ref, b_ref, a_ref, fe_ref, fw_ref, base_ref, top_ref, air_ref, sea_ref, fb_s, fo_s, fa_s, b_s, a_s):
    sea_ref[...] = base_ref[...]
    sea_ref[0:8, :] = top_ref[0:8, :]
    sea_ref[NSEA : NSEA + 4, :] = top_ref[8:12, :]
    o0, o1 = NMSG, NMSG + NOWN
    fb_s[...] = beyond(fe_ref[:, 0:o0], fw_ref[:, 0:o0])
    fo_s[...] = beyond(fe_ref[:, o0:o1], fw_ref[:, o0:o1])
    fa_s[...] = beyond(fe_ref[:, o1:], fw_ref[:, o1:])
    b_s[...] = b_ref[0:NAIR, :].astype(f32)
    a_s[...] = a_ref[0:NAIR, :].astype(f32)

    def chunk(i, _):
        at = i * 8 * ROWS

        def take(ref, start):
            return ref[pl.ds(start + at, 8, stride=ROWS), :]

        fields = []
        for k in range(3):
            rows = []
            for r in range(ROWS):
                rows.append((take(b_s, k * NA1 + r), take(fb_s, k * NA1 + r)))
            for r in range(ROWS):
                own = take(q_ref, r) if k == 0 else take(c_ref, (k - 1) * NA1 + r)
                rows.append((own, take(fo_s, k * NA1 + r)))
            for r in range(ROWS):
                rows.append((take(a_s, k * NA1 + r), take(fa_s, k * NA1 + r)))
            fields.append([jnp.concatenate(p, axis=1) for p in rows])
        q, cx, cy = fields
        for step in range(NSTEP):
            n = len(q)
            north = []
            for j in range(n - 1):
                g = cy[step + j]
                north.append(jnp.maximum(g, 0.0) * q[j] + jnp.minimum(g, 0.0) * q[j + 1])
            new = []
            for j in range(1, n - 1):
                g = cx[step + j]
                east = jnp.maximum(g, 0.0) * q[j] + jnp.minimum(g, 0.0) * pltpu.roll(q[j], 2 * COLS - 1, 1)
                new.append(q[j] - (east - pltpu.roll(east, 1, 1)) - (north[j] - north[j - 1]))
            q = new
        for r in range(ROWS):
            air_ref[pl.ds(at + r, 8, stride=ROWS), :] = q[r][:, :COLS]
        return 0

    lax.fori_loop(0, LEV // 8, chunk, 0)


def back_kernel(ntile, came_ref, w_ref, tc_ref, tr_ref, out_ref):
    tcol, _, rank_col, _ = entry_tables(tc_ref, tr_ref)
    at = tcol * 4 + rank_col * 2
    lane = iota((PADE, 4 * ntile), 1)
    want = jnp.concatenate([onehot(lane == at), onehot(lane == at + 1)], axis=0)
    values = dot(want, came_ref[...], 1, 0)
    values = jnp.concatenate([values, jnp.ones((16, COLS), f32)], axis=0).astype(bf16)
    pairs = dot(values, w_ref[...], 1, 1)
    e, l = iota((PADE, SUB * ENTS), 0), iota((PADE, SUB * ENTS), 1)
    mine = l // SUB == e
    sums = [
        jnp.sum(jnp.where(mine, pairs[c * PADE : (c + 1) * PADE], 0.0), axis=0, keepdims=True) for c in range(2)
    ] + [pairs[2 * PADE : 2 * PADE + 1]]
    wide = 3 * COLS
    stack = jnp.concatenate([s[:, r * wide : (r + 1) * wide] for s in sums for r in range(ROWS)] + [jnp.ones((4, wide), f32)], axis=0)
    src, dst = iota((wide, COLS), 0), iota((wide, COLS), 1)
    move = jnp.where((src % SUB == dst % SUB) & ((src // SUB) // OVL == dst // SUB), 1.0, 0.0)
    moved = dot(stack, move, 1, 0, precision=lax.Precision.HIGHEST)
    areas = moved[8:12]
    out_ref[...] = moved[0:8] / jnp.concatenate([areas, areas], axis=0)


def body(
    atmosphere_tracer_state,
    courant,
    surface_exchange_factor,
    prior_sea_surface_temper,
    remap_overlay_weight,
    remap_dest_tile,
    remap_dest_block,
    ocean_level_state,
    ocean_cell_mask,
):
    ntile = lax.axis_size("tile")
    sds = jax.ShapeDtypeStruct
    q = atmosphere_tracer_state.reshape(NA1, COLS)
    c = courant.reshape(2 * NA1, COLS)
    x = ocean_level_state.reshape(2 * NSEA, COLS)
    mask = ocean_cell_mask
    weights = remap_overlay_weight.reshape(ENTS * SUB, COLS)
    tiles = jnp.pad(remap_dest_tile[0], (0, PADE - ENTS), constant_values=-1000)
    blocks = jnp.pad(remap_dest_block[0], (0, PADE - ENTS))
    tcol, bcol = tiles[:, None], blocks[:, None]
    trow = jnp.tile(tiles, 4)[None, :]

    msg = sds((NMSG, COLS), bf16)
    up, down = call(pack_kernel, (msg, msg), q, c, x, mask)
    before = lax.ppermute(up, "comp", ring("comp", 1))
    after = lax.ppermute(down, "comp", ring("comp", -1))
    strip = sds((8, NSTR), bf16)
    west, east = call(strip_kernel, (strip, strip), q, c, x, mask, before, after)
    fe = lax.ppermute(west, "tile", ring("tile", -1))
    fw = lax.ppermute(east, "tile", ring("tile", 1))

    slots = sds((4 * ntile, COLS), bf16)
    outgoing = call(
        functools.partial(flux_kernel, ntile), slots,
        q, c, before, after, fe, fw, surface_exchange_factor, prior_sea_surface_temper, weights, tcol, trow, bcol,
    )
    outgoing, fe1 = lax.optimization_barrier((outgoing, fe))

    def exchange(a):
        a = a.reshape(ntile, 4, COLS)
        return lax.all_to_all(a, "tile", split_axis=0, concat_axis=0, tiled=True).reshape(4 * ntile, COLS)

    far = [pltpu.VMEM((n, COLS), f32) for n in (NMSG, NOWN, NMSG)]
    arrived = exchange(outgoing)
    base, wide_wet = call(
        sea_kernel, (sds((2 * NSEA, COLS), f32), sds((8, 2 * COLS), f32)),
        x, mask, before, after, fe1, fw, scratch=[pltpu.VMEM((2 * NSEA + 16, COLS), f32)] + far,
    )
    tile8 = sds((8, COLS), f32)
    aux, keep, to_up, to_down = call(
        functools.partial(force_kernel, ntile), (sds((ntile, COLS), bf16), sds((16, COLS), f32), tile8, tile8),
        arrived, wide_wet, scratch=[pltpu.VMEM((4 * ntile, COLS), f32)],
    )
    below = lax.ppermute(to_up, "comp", ring("comp", 1))
    above = lax.ppermute(to_down, "comp", ring("comp", -1))
    sent, top = call(
        functools.partial(surface_kernel, ntile), (slots, sds((16, COLS), f32)),
        base, keep, below, above, aux, scratch=[pltpu.VMEM((4 * ntile, COLS), f32)],
    )
    sent, top = lax.optimization_barrier((sent, top))
    came = exchange(sent)
    air_new, ocean_new = call(
        air_kernel, (sds((NA1, COLS), f32), sds((2 * NSEA, COLS), f32)),
        q, c, before, after, fe, fw, base, top, scratch=far + [pltpu.VMEM((NAIR, COLS), f32)] * 2,
    )
    surface_air = call(functools.partial(back_kernel, ntile), tile8, came, weights, tcol, trow)
    return (
        air_new.reshape(atmosphere_tracer_state.shape),
        ocean_new.reshape(ocean_level_state.shape),
        surface_air.reshape(2, ROWS, COLS),
    )


def solution(mesh):
    return jax.shard_map(
        body,
        mesh=mesh,
        in_specs=(
            P(None, "comp", "tile"),
            P(None, None, "comp", "tile"),
            P("comp", "tile"),
            P("comp", "tile"),
            P("comp", "tile", None, None),
            P("comp", "tile"),
            P("comp", "tile"),
            P(None, None, "comp", "tile"),
            P("comp", "tile"),
        ),
        out_specs=(P(None, "comp", "tile"), P(None, None, "comp", "tile"), P(None, "comp", "tile")),
        check_vma=False,
    )
```

```python
import functools

import jax
import jax.numpy as jnp
from jax import lax
from jax.experimental import pallas as pl
from jax.experimental.pallas import tpu as pltpu
from jax.sharding import PartitionSpec as P

OVL = 3
NSTEP = 4
NOSTEP = 2
INTERPRET = False

hor_mix = 0.12
vert_mix = 0.2
press_grad = 0.3


bf16 = jnp.bfloat16
f32 = jnp.float32
i32 = jnp.int32

LEV, OL, ROWS, COLS, SUB, ENTS = 72, 62, 4, 128, 32, 48
NAIR = 3 * LEV * ROWS
NA1 = LEV * ROWS
NSEA = OL * ROWS
OLP = 64
SEA0 = NAIR
WET0 = SEA0 + 4 * OLP
LOW0 = WET0 + 16
NMSG = LOW0 + 16
OSEA0 = NAIR
OWET0 = OSEA0 + 2 * NSEA
OLOW0 = OWET0 + 16
NOWN = OLOW0 + 32
NSTR = 2 * NMSG + NOWN
PADE = 64


def dot(a, b, ca, cb, **kw):
    return lax.dot_general(a, b, (((ca,), (cb,)), ((), ())), preferred_element_type=f32, **kw)


def iota(shape, axis):
    return lax.broadcasted_iota(i32, shape, axis)


def onehot(mask):
    return jnp.where(mask, 1.0, 0.0).astype(bf16)


def call(kernel, outs, *args, scratch=(), far=0):
    vmem = pl.BlockSpec(memory_space=pltpu.VMEM)
    specs = [pl.BlockSpec(memory_space=pltpu.HBM)] * far + [vmem] * (len(args) - far)
    return pl.pallas_call(
        kernel,
        out_shape=outs,
        in_specs=specs,
        scratch_shapes=list(scratch),
        compiler_params=None if INTERPRET else pltpu.CompilerParams(vmem_limit_bytes=48 << 20),
        interpret=INTERPRET,
    )(*args)


def ring(axis, step):
    size = lax.axis_size(axis)
    return [(i, (i + step) % size) for i in range(size)]


def low_rows(q_ref, c_ref):
    pieces = [q_ref[NA1 - 4 : NA1, :], c_ref[NA1 - 4 : NA1, :], c_ref[2 * NA1 - 4 : 2 * NA1, :]]
    return jnp.concatenate(pieces + [jnp.zeros((4, COLS), f32)], axis=0).astype(bf16)


def pack_kernel(q_hbm, c_hbm, x_hbm, m_hbm, up_ref, down_ref, q_ref, c_ref, x_ref, m_ref, sem):
    pairs = ((q_hbm, q_ref), (c_hbm, c_ref), (x_hbm, x_ref), (m_hbm, m_ref))
    copies = [pltpu.make_async_copy(src, dst, sem.at[i]) for i, (src, dst) in enumerate(pairs)]
    for copy in copies:
        copy.start()
    for copy in copies:
        copy.wait()
    q = q_ref[...].astype(bf16)
    c = c_ref[...].astype(bf16)
    low = low_rows(q_ref, c_ref)
    mask = m_ref[...].astype(f32)
    for ref, r0, mr in ((up_ref, ROWS - 2, ROWS - 1), (down_ref, 0, 0)):
        ref[0:NA1, :] = q
        ref[NA1:NAIR, :] = c
        for v in range(2):
            for r in range(2):
                at = SEA0 + (2 * v + r) * OLP
                part = x_ref[pl.ds(v * NSEA + r0 + r, OL, stride=ROWS), :]
                ref[at : at + OLP, :] = jnp.concatenate([part, jnp.zeros((OLP - OL, COLS), f32)], axis=0).astype(bf16)
        ref[WET0:LOW0, :] = jnp.broadcast_to(mask[mr : mr + 1], (16, COLS)).astype(bf16)
        ref[LOW0:NMSG, :] = low


def place_matrix(first):
    j, lane = iota((8, COLS), 0), iota((8, COLS), 1)
    return onehot((j < 4) & (lane == (j if first else j + COLS - 4)))


def strip_kernel(q_ref, c_ref, x_ref, m_ref, b_ref, a_ref, west_ref, east_ref):
    mask = jnp.concatenate([m_ref[...].astype(f32), jnp.zeros((12, COLS), f32)], axis=0).astype(bf16)
    tail = jnp.concatenate([mask, low_rows(q_ref, c_ref), jnp.zeros((16, COLS), bf16)], axis=0)
    own = jnp.concatenate([q_ref[...].astype(bf16), c_ref[...].astype(bf16), x_ref[...].astype(bf16), tail], axis=0)
    for ref, first in ((west_ref, True), (east_ref, False)):
        place = place_matrix(first)
        ref[:, 0:NMSG] = dot(place, b_ref[...], 1, 1).astype(bf16)
        ref[:, NMSG : NMSG + NOWN] = dot(place, own, 1, 1).astype(bf16)
        ref[:, NMSG + NOWN :] = dot(place, a_ref[...], 1, 1).astype(bf16)


def beyond(fe, fw):
    both = fe.astype(f32) + pltpu.roll(fw.astype(f32), 4, 0)
    j, lane = iota((8, COLS), 0), iota((8, COLS), 1)
    place = jnp.where(lane == jnp.where(j < 4, j, j + COLS - 8), 1.0, 0.0)
    return dot(both, place, 0, 0)


def entry_tables(tc_ref, tr_ref):
    tcol = tc_ref[...]
    trow = tr_ref[...]
    e, l = iota((PADE, 4 * PADE), 0), iota((PADE, 4 * PADE), 1)
    same = tcol == trow
    rank_row = jnp.sum(jnp.where(same & (e < l % PADE), 1, 0), axis=0, keepdims=True)
    rank_col = jnp.sum(jnp.where(same & (l < e), 1, 0), axis=1, keepdims=True)
    return tcol, trow, rank_col, rank_row


def flux_kernel(q_ref, c_ref, b_ref, a_ref, fe_ref, fw_ref, f_ref, p_ref, w_ref, spread_ref, mask_ref, out_ref):
    parts = []
    mine = (q_ref[NA1 - 4 : NA1, :], c_ref[NA1 - 4 : NA1, :], c_ref[2 * NA1 - 4 : 2 * NA1, :])
    nb = b_ref[LOW0:NMSG, :].astype(f32)
    na = a_ref[LOW0:NMSG, :].astype(f32)
    lo_b = beyond(fe_ref[:, NMSG - COLS : NMSG], fw_ref[:, NMSG - COLS : NMSG])[COLS - 16 :]
    o1 = NMSG + NOWN
    lo_o = beyond(fe_ref[:, o1 - COLS : o1], fw_ref[:, o1 - COLS : o1])[COLS - 32 : COLS - 16]
    lo_a = beyond(fe_ref[:, NSTR - COLS :], fw_ref[:, NSTR - COLS :])[COLS - 16 :]
    pad = jnp.zeros((4, COLS), f32)
    for i in range(3):
        s = slice(4 * i, 4 * i + 4)
        main = jnp.concatenate([nb[s], mine[i], na[s], pad], axis=0)
        far = jnp.concatenate([lo_b[s], lo_o[s], lo_a[s], pad], axis=0)
        parts.append(jnp.concatenate([main, far], axis=1))
    q, cx, cy = parts
    xp, xm, yp, ym = jnp.maximum(cx, 0.0), jnp.minimum(cx, 0.0), jnp.maximum(cy, 0.0), jnp.minimum(cy, 0.0)
    aw, xm_w = pltpu.roll(xp, 1, 1), pltpu.roll(xm, 1, 1)
    a_s, ym_s = pltpu.roll(yp, 1, 0), pltpu.roll(ym, 1, 0)
    a0 = 1.0 - xp + xm_w - yp + ym_s
    for _ in range(NSTEP):
        west, east = pltpu.roll(q, 1, 1), pltpu.roll(q, 2 * COLS - 1, 1)
        south, north = pltpu.roll(q, 1, 0), pltpu.roll(q, 15, 0)
        q = (a0 * q + aw * west - xm * east) + (a_s * south - ym * north)
    flux = f_ref[...] * (q[ROWS : 2 * ROWS, :COLS] - p_ref[...])
    flux = jnp.concatenate([flux, jnp.zeros((4, COLS), f32)], axis=0).astype(bf16).astype(f32)
    turned = jnp.concatenate([flux] + [pltpu.roll(flux, SUB * d, 1) for d in range(1, 4)], axis=0).astype(bf16)
    e, k = iota((PADE, 32), 0), iota((PADE, 32), 1)
    turn = (e % 4 - (e // 3) % 4 + 4) % 4
    pick = onehot((e < ENTS) & (k == turn * 8 + e // 12))
    lined = dot(pick, turned, 1, 0)
    e, lane = iota((PADE, COLS), 0), iota((PADE, COLS), 1)
    lined = jnp.where(lane // SUB == e % 4, lined, 0.0)
    spread_flux = jnp.concatenate([jnp.where(e // 4 == j, lined, 0.0) for j in range(ENTS // 4)], axis=1).astype(bf16)
    contrib = dot(spread_flux, w_ref[...], 1, 0).astype(bf16).astype(f32)
    west = mask_ref[PADE : 2 * PADE, :] * contrib[:, COLS - 1 :]
    east = mask_ref[2 * PADE :, :] * contrib[:, :1]
    table = jnp.concatenate([contrib, mask_ref[0:PADE, :], west, east], axis=0).astype(bf16)
    out_ref[...] = dot(spread_ref[...], table, 1, 0).astype(bf16)


def line_up(sums):
    wide = 3 * COLS
    rows = [s[:, r * wide : (r + 1) * wide] for s in sums for r in range(ROWS)]
    stack = jnp.concatenate(rows + [jnp.zeros((8 - len(rows), wide), f32)] * (len(rows) < 8), axis=0)
    src, dst = iota((wide, COLS), 0), iota((wide, COLS), 1)
    move = jnp.where((src % SUB == dst % SUB) & ((src // SUB) // OVL == dst // SUB), 1.0, 0.0)
    return dot(stack, move, 1, 0, precision=lax.Precision.HIGHEST)


def table_kernel(ntile, tc_ref, tr_ref, bc_ref, w_ref, spread_ref, mask_ref, want_ref, area_ref):
    tcol, trow, rank_col, rank_row = entry_tables(tc_ref, tr_ref)
    lane = iota((PADE, COLS), 1)
    hit = (lane % 4 == bc_ref[...]) & ((lane // 4) % 2 == rank_col)
    spans = ((0, 16), (16, 24), (24, 32))
    mask_ref[...] = jnp.concatenate([jnp.where(hit & (lane >= a) & (lane < b), 1.0, 0.0) for a, b in spans], axis=0)
    kind = iota((1, 4 * PADE), 1) // PADE
    to = jnp.where(kind == 2, jnp.where(trow == ntile - 1, 0, trow + 1), trow)
    to = jnp.where(kind == 3, jnp.where(trow == 0, ntile - 1, trow - 1), to)
    slot = jnp.where(kind == 0, rank_row, 2)
    spread_ref[...] = onehot(iota((4 * ntile, 4 * PADE), 0) == to * 4 + slot)
    at = tcol * 4 + rank_col * 2
    col = iota((PADE, 4 * ntile), 1)
    want_ref[...] = jnp.concatenate([onehot(col == at), onehot(col == at + 1)], axis=0)
    areas = line_up([dot(jnp.ones((16, COLS), bf16), w_ref[...], 1, 1)[0:1]])[0:4]
    area_ref[...] = jnp.concatenate([areas, areas], axis=0)


def sea_kernel(x_ref, m_ref, b_ref, a_ref, fe_ref, fw_ref, out_ref, wide_ref, x_s, fb_s, fo_s, fa_s):
    o0, o1 = NMSG, NMSG + NOWN
    fb_s[...] = beyond(fe_ref[:, 0:o0], fw_ref[:, 0:o0])
    fo_s[...] = beyond(fe_ref[:, o0:o1], fw_ref[:, o0:o1])
    fa_s[...] = beyond(fe_ref[:, o1:], fw_ref[:, o1:])
    x_s[0 : 2 * NSEA, :] = x_ref[...]
    x_s[2 * NSEA :, :] = jnp.zeros((16, COLS), f32)

    def join(main, far):
        return jnp.concatenate([main, far], axis=1)

    wet = [join(b_ref[WET0 : WET0 + 16, :].astype(f32)[:1], fb_s[WET0 : WET0 + 1, :])]
    mask = m_ref[...].astype(f32)
    for r in range(ROWS):
        wet.append(join(mask[r : r + 1], fo_s[OWET0 + r : OWET0 + r + 1, :]))
    wet.append(join(a_ref[WET0 : WET0 + 16, :].astype(f32)[:1], fa_s[WET0 : WET0 + 1, :]))
    wide_ref[...] = jnp.concatenate(wet + [jnp.zeros((2, 2 * COLS), f32)], axis=0)
    level = iota((OLP, 2 * COLS), 0)
    top, bottom = level == 0, level >= OL - 1

    state = []
    for v in range(2):
        rows = []
        for r in range(2):
            at = SEA0 + (2 * v + r) * OLP
            rows.append(join(b_ref[at : at + OLP, :].astype(f32), fb_s[at : at + OLP, :]))
        for r in range(ROWS):
            at = v * NSEA + r
            rows.append(join(x_s[pl.ds(at, OLP, stride=ROWS), :], fo_s[pl.ds(OSEA0 + at, OLP, stride=ROWS), :]))
        for r in range(2):
            at = SEA0 + (2 * v + r) * OLP
            rows.append(join(a_ref[at : at + OLP, :].astype(f32), fa_s[at : at + OLP, :]))
        state.append(rows)
    for step in range(NOSTEP):
        new = [[], []]
        for j in range(1, len(state[0]) - 1):
            w = wet[j - 1 + step]
            for v in range(2):
                mid = state[v][j]
                ahead, behind = pltpu.roll(mid, 2 * COLS - 1, 1), pltpu.roll(mid, 1, 1)
                lap = state[v][j + 1] + state[v][j - 1] + ahead + behind - 4.0 * mid
                under = jnp.where(bottom, 0.0, pltpu.roll(mid, OLP - 1, 0) - mid)
                over = jnp.where(top, 0.0, mid - pltpu.roll(mid, 1, 0))
                tend = hor_mix * lap + vert_mix * (under - over)
                if v == 0:
                    gradient = ahead - behind
                else:
                    tend = tend - press_grad * gradient
                new[v].append(mid + w * tend)
        state = new
    for v in range(2):
        for r in range(ROWS):
            out_ref[pl.ds(v * NSEA + r, OL, stride=ROWS), :] = state[v][r][:OL, :COLS]


def force_kernel(ntile, got_ref, wide_ref, aux_ref, keep_ref, up_ref, down_ref, s_ref):
    s_ref[...] = got_ref[...].astype(f32)
    first = s_ref[pl.ds(0, ntile, stride=4), :].astype(bf16)
    second = s_ref[pl.ds(1, ntile, stride=4), :].astype(bf16)
    aux32 = s_ref[pl.ds(2, ntile, stride=4), :]
    aux = aux32.astype(bf16)
    aux_ref[...] = aux
    force = dot(aux32, first.astype(f32), 0, 0)[0:4] + dot(aux32, second.astype(f32), 0, 0)[4:8]
    sums = jnp.sum(aux32, axis=0, keepdims=True)
    r, lane = iota((ROWS, COLS), 0), iota((ROWS, COLS), 1)
    mine = lane % 4 == r
    west = jnp.sum(jnp.where(mine & (lane >= 16) & (lane < 24), sums, 0.0), axis=1, keepdims=True)
    east = jnp.sum(jnp.where(mine & (lane >= 24) & (lane < 32), sums, 0.0), axis=1, keepdims=True)
    wet = wide_ref[1 : ROWS + 1, :]
    pushed = wet[:, :COLS] * force
    west = wet[:, 2 * COLS - 1 :] * west
    east = wet[:, COLS : COLS + 1] * east
    ahead = jnp.where(lane == COLS - 1, east, pltpu.roll(jnp.concatenate([pushed, pushed], axis=0), COLS - 1, 1)[:ROWS])
    behind = jnp.where(lane == 0, west, pltpu.roll(jnp.concatenate([pushed, pushed], axis=0), 1, 1)[:ROWS])
    keep_ref[...] = jnp.concatenate([pushed, ahead, behind, wet[:, :COLS]], axis=0)
    up_ref[...] = jnp.broadcast_to(pushed[ROWS - 1 :], (8, COLS))
    down_ref[...] = jnp.broadcast_to(pushed[:1], (8, COLS))


def surface_kernel(ntile, base_ref, keep_ref, below_ref, above_ref, aux_ref, sent_ref, top_ref, s_ref):
    pushed, ahead, behind = keep_ref[0:4, :], keep_ref[4:8, :], keep_ref[8:12, :]
    wet = keep_ref[12:16, :]
    upper = jnp.concatenate([pushed[1:], above_ref[0:1, :]], axis=0)
    lower = jnp.concatenate([below_ref[0:1, :], pushed[:-1]], axis=0)
    lap = upper + lower + ahead + behind - 4.0 * pushed
    temp0 = base_ref[0:4, :] + (2.0 * pushed + wet * (hor_mix * lap - vert_mix * pushed))
    temp1 = base_ref[4:8, :] + wet * (vert_mix * pushed)
    cur0 = base_ref[NSEA : NSEA + 4, :] - wet * (press_grad * (ahead - behind))
    top_ref[...] = jnp.concatenate([temp0, temp1, cur0, jnp.zeros((4, COLS), f32)], axis=0)
    table = jnp.concatenate([temp0, temp0, cur0, cur0], axis=0)
    row = iota((16, COLS), 0)
    aux = aux_ref[...][:, :16]
    for slot in range(2):
        for c in range(2):
            part = jnp.where(row // 4 == 2 * c + slot, table, 0.0).astype(bf16)
            s_ref[pl.ds(2 * slot + c, ntile, stride=4), :] = dot(aux, part, 1, 0)
    sent_ref[...] = s_ref[...].astype(bf16)


def air_kernel(q_ref, c_ref, b_ref, a_ref, fe_ref, fw_ref, base_ref, top_ref, air_ref, sea_ref, fb_s, fo_s, fa_s, b_s, a_s):
    sea_ref[...] = base_ref[...]
    sea_ref[0:8, :] = top_ref[0:8, :]
    sea_ref[NSEA : NSEA + 4, :] = top_ref[8:12, :]
    o0, o1 = NMSG, NMSG + NOWN
    fb_s[...] = beyond(fe_ref[:, 0:o0], fw_ref[:, 0:o0])
    fo_s[...] = beyond(fe_ref[:, o0:o1], fw_ref[:, o0:o1])
    fa_s[...] = beyond(fe_ref[:, o1:], fw_ref[:, o1:])
    b_s[...] = b_ref[0:NAIR, :].astype(f32)
    a_s[...] = a_ref[0:NAIR, :].astype(f32)

    def chunk(i, _):
        at = i * 8 * ROWS

        def take(ref, start):
            return ref[pl.ds(start + at, 8, stride=ROWS), :]

        fields = []
        for k in range(3):
            rows = []
            for r in range(ROWS):
                rows.append((take(b_s, k * NA1 + r), take(fb_s, k * NA1 + r)))
            for r in range(ROWS):
                own = take(q_ref, r) if k == 0 else take(c_ref, (k - 1) * NA1 + r)
                rows.append((own, take(fo_s, k * NA1 + r)))
            for r in range(ROWS):
                rows.append((take(a_s, k * NA1 + r), take(fa_s, k * NA1 + r)))
            fields.append([jnp.concatenate(p, axis=1) for p in rows])
        q, cx, cy = fields
        yp, ym = [jnp.maximum(g, 0.0) for g in cy], [jnp.minimum(g, 0.0) for g in cy]
        coefs = [None]
        for j in range(1, 3 * ROWS - 1):
            xp, xm = jnp.maximum(cx[j], 0.0), jnp.minimum(cx[j], 0.0)
            coefs.append((1.0 - xp + pltpu.roll(xm, 1, 1) - yp[j] + ym[j - 1], pltpu.roll(xp, 1, 1), xm))
        for step in range(NSTEP):
            new = []
            for j in range(1, len(q) - 1):
                a0, aw, xm = coefs[step + j]
                west, east = pltpu.roll(q[j], 1, 1), pltpu.roll(q[j], 2 * COLS - 1, 1)
                rest = yp[step + j - 1] * q[j - 1] - ym[step + j] * q[j + 1]
                new.append((a0 * q[j] + aw * west - xm * east) + rest)
            q = new
        for r in range(ROWS):
            air_ref[pl.ds(at + r, 8, stride=ROWS), :] = q[r][:, :COLS]
        return 0

    lax.fori_loop(0, LEV // 8, chunk, 0)


def back_kernel(came_ref, w_ref, want_ref, area_ref, out_ref):
    values = dot(want_ref[...], came_ref[...], 1, 0).astype(bf16)
    pairs = dot(values, w_ref[...], 1, 1)
    e, l = iota((PADE, SUB * ENTS), 0), iota((PADE, SUB * ENTS), 1)
    mine = l // SUB == e
    halves = (pairs[:PADE], pairs[PADE:])
    sums = [jnp.sum(jnp.where(mine, h, 0.0), axis=0, keepdims=True) for h in halves]
    out_ref[...] = line_up(sums) / area_ref[...]


def body(
    atmosphere_tracer_state,
    courant,
    surface_exchange_factor,
    prior_sea_surface_temper,
    remap_overlay_weight,
    remap_dest_tile,
    remap_dest_block,
    ocean_level_state,
    ocean_cell_mask,
):
    ntile = lax.axis_size("tile")
    sds = jax.ShapeDtypeStruct
    q = atmosphere_tracer_state.reshape(NA1, COLS)
    c = courant.reshape(2 * NA1, COLS)
    x = ocean_level_state.reshape(2 * NSEA, COLS)
    mask = ocean_cell_mask
    weights = remap_overlay_weight.reshape(ENTS * SUB, COLS)
    tiles = jnp.pad(remap_dest_tile[0], (0, PADE - ENTS), constant_values=-1000)
    blocks = jnp.pad(remap_dest_block[0], (0, PADE - ENTS))
    tcol, bcol = tiles[:, None], blocks[:, None]
    trow = jnp.tile(tiles, 4)[None, :]

    msg = sds((NMSG, COLS), bf16)
    stay = (lambda a: a) if INTERPRET else (lambda a: pltpu.with_memory_space_constraint(a, pltpu.HBM))
    up, down = call(
        pack_kernel, (msg, msg), *[stay(a) for a in (q, c, x, mask)], far=4,
        scratch=[pltpu.VMEM(a.shape, a.dtype) for a in (q, c, x, mask)] + [pltpu.SemaphoreType.DMA((4,))],
    )
    before = lax.ppermute(up, "comp", ring("comp", 1))
    after = lax.ppermute(down, "comp", ring("comp", -1))
    strip = sds((8, NSTR), bf16)
    west, east = call(strip_kernel, (strip, strip), q, c, x, mask, before, after)
    slots = sds((4 * ntile, COLS), bf16)
    tcol, west, east = lax.optimization_barrier((tcol, west, east))
    fe = lax.ppermute(west, "tile", ring("tile", -1))
    fw = lax.ppermute(east, "tile", ring("tile", 1))
    spread, masks, want, areas = call(
        functools.partial(table_kernel, ntile),
        (sds((4 * ntile, 4 * PADE), bf16), sds((3 * PADE, COLS), f32), sds((2 * PADE, 4 * ntile), bf16), sds((8, COLS), f32)),
        tcol, trow, bcol, weights,
    )
    outgoing = call(
        flux_kernel, slots,
        q, c, before, after, fe, fw, surface_exchange_factor, prior_sea_surface_temper, weights, spread, masks,
    )
    outgoing, fe1 = lax.optimization_barrier((outgoing, fe))

    def exchange(a):
        a = a.reshape(ntile, 4, COLS)
        return lax.all_to_all(a, "tile", split_axis=0, concat_axis=0, tiled=True).reshape(4 * ntile, COLS)

    far = [pltpu.VMEM((n, COLS), f32) for n in (NMSG, NOWN, NMSG)]
    arrived = exchange(outgoing)
    base, wide_wet = call(
        sea_kernel, (sds((2 * NSEA, COLS), f32), sds((8, 2 * COLS), f32)),
        x, mask, before, after, fe1, fw, scratch=[pltpu.VMEM((2 * NSEA + 16, COLS), f32)] + far,
    )
    tile8 = sds((8, COLS), f32)
    aux, keep, to_up, to_down = call(
        functools.partial(force_kernel, ntile), (sds((ntile, COLS), bf16), sds((16, COLS), f32), tile8, tile8),
        arrived, wide_wet, scratch=[pltpu.VMEM((4 * ntile, COLS), f32)],
    )
    below = lax.ppermute(to_up, "comp", ring("comp", 1))
    above = lax.ppermute(to_down, "comp", ring("comp", -1))
    sent, top = call(
        functools.partial(surface_kernel, ntile), (slots, sds((16, COLS), f32)),
        base, keep, below, above, aux, scratch=[pltpu.VMEM((4 * ntile, COLS), f32)],
    )
    sent, top = lax.optimization_barrier((sent, top))
    came = exchange(sent)
    air_new, ocean_new = call(
        air_kernel, (sds((NA1, COLS), f32), sds((2 * NSEA, COLS), f32)),
        q, c, before, after, fe, fw, base, top, scratch=far + [pltpu.VMEM((NAIR, COLS), f32)] * 2,
    )
    surface_air = call(back_kernel, tile8, came, weights, want, areas)
    return (
        air_new.reshape(atmosphere_tracer_state.shape),
        ocean_new.reshape(ocean_level_state.shape),
        surface_air.reshape(2, ROWS, COLS),
    )


def solution(mesh):
    return jax.shard_map(
        body,
        mesh=mesh,
        in_specs=(
            P(None, "comp", "tile"),
            P(None, None, "comp", "tile"),
            P("comp", "tile"),
            P("comp", "tile"),
            P("comp", "tile", None, None),
            P("comp", "tile"),
            P("comp", "tile"),
            P(None, None, "comp", "tile"),
            P("comp", "tile"),
        ),
        out_specs=(P(None, "comp", "tile"), P(None, None, "comp", "tile"), P(None, "comp", "tile")),
        check_vma=False,
    )
```

```python
import functools

import jax
import jax.numpy as jnp
from jax import lax
from jax.experimental import pallas as pl
from jax.experimental.pallas import tpu as pltpu
from jax.sharding import PartitionSpec as P

OVL = 3
NSTEP = 4
NOSTEP = 2
INTERPRET = False

hor_mix = 0.12
vert_mix = 0.2
press_grad = 0.3


bf16 = jnp.bfloat16
f32 = jnp.float32
i32 = jnp.int32

LEV, OL, ROWS, COLS, SUB, ENTS = 72, 62, 4, 128, 32, 48
NAIR = 3 * LEV * ROWS
NA1 = LEV * ROWS
NSEA = OL * ROWS
OLP = 64
SEA0 = NAIR
WET0 = SEA0 + 4 * OLP
LOW0 = WET0 + 16
NMSG = LOW0 + 16
OSEA0 = NAIR
OWET0 = OSEA0 + 2 * NSEA
OLOW0 = OWET0 + 16
NOWN = OLOW0 + 32
NSTR = 2 * NMSG + NOWN
PADE = 64
NY = 4


def dot(a, b, ca, cb, **kw):
    return lax.dot_general(a, b, (((ca,), (cb,)), ((), ())), preferred_element_type=f32, **kw)


def iota(shape, axis):
    return lax.broadcasted_iota(i32, shape, axis)


def onehot(mask):
    return jnp.where(mask, 1.0, 0.0).astype(bf16)


def call(kernel, outs, *args, scratch=(), far=0, smem=0):
    vmem = pl.BlockSpec(memory_space=pltpu.VMEM)
    specs = [pl.BlockSpec(memory_space=pltpu.HBM)] * far + [pl.BlockSpec(memory_space=pltpu.SMEM)] * smem
    specs += [vmem] * (len(args) - len(specs))
    return pl.pallas_call(
        kernel,
        out_shape=outs,
        in_specs=specs,
        scratch_shapes=list(scratch),
        compiler_params=None if INTERPRET else pltpu.CompilerParams(vmem_limit_bytes=48 << 20),
        interpret=INTERPRET,
    )(*args)


def ring(axis, step):
    size = lax.axis_size(axis)
    return [(i, (i + step) % size) for i in range(size)]


def low_rows(q_ref, c_ref):
    pieces = [q_ref[NA1 - 4 : NA1, :], c_ref[NA1 - 4 : NA1, :], c_ref[2 * NA1 - 4 : 2 * NA1, :]]
    return jnp.concatenate(pieces + [jnp.zeros((4, COLS), f32)], axis=0).astype(bf16)


def pack_kernel(q_hbm, c_hbm, x_hbm, m_hbm, up_ref, down_ref, q_ref, c_ref, x_ref, m_ref, sem):
    pairs = ((q_hbm, q_ref), (c_hbm, c_ref), (x_hbm, x_ref), (m_hbm, m_ref))
    copies = [pltpu.make_async_copy(src, dst, sem.at[i]) for i, (src, dst) in enumerate(pairs)]
    for copy in copies:
        copy.start()
    for copy in copies:
        copy.wait()
    q = q_ref[...].astype(bf16)
    c = c_ref[...].astype(bf16)
    low = low_rows(q_ref, c_ref)
    mask = m_ref[...].astype(f32)
    for ref, r0, mr in ((up_ref, ROWS - 2, ROWS - 1), (down_ref, 0, 0)):
        ref[0:NA1, :] = q
        ref[NA1:NAIR, :] = c
        for v in range(2):
            for r in range(2):
                at = SEA0 + (2 * v + r) * OLP
                part = x_ref[pl.ds(v * NSEA + r0 + r, OL, stride=ROWS), :]
                ref[at : at + OLP, :] = jnp.concatenate([part, jnp.zeros((OLP - OL, COLS), f32)], axis=0).astype(bf16)
        ref[WET0:LOW0, :] = jnp.broadcast_to(mask[mr : mr + 1], (16, COLS)).astype(bf16)
        ref[LOW0:NMSG, :] = low


def place_matrix(first):
    j, lane = iota((8, COLS), 0), iota((8, COLS), 1)
    return onehot((j < 4) & (lane == (j if first else j + COLS - 4)))


def strip_kernel(q_ref, c_ref, x_ref, m_ref, b_ref, a_ref, west_ref, east_ref):
    mask = jnp.concatenate([m_ref[...].astype(f32), jnp.zeros((12, COLS), f32)], axis=0).astype(bf16)
    tail = jnp.concatenate([mask, low_rows(q_ref, c_ref), jnp.zeros((16, COLS), bf16)], axis=0)
    own = jnp.concatenate([q_ref[...].astype(bf16), c_ref[...].astype(bf16), x_ref[...].astype(bf16), tail], axis=0)
    for ref, first in ((west_ref, True), (east_ref, False)):
        place = place_matrix(first)
        ref[:, 0:NMSG] = dot(place, b_ref[...], 1, 1).astype(bf16)
        ref[:, NMSG : NMSG + NOWN] = dot(place, own, 1, 1).astype(bf16)
        ref[:, NMSG + NOWN :] = dot(place, a_ref[...], 1, 1).astype(bf16)


def beyond(fe, fw):
    both = fe.astype(f32) + pltpu.roll(fw.astype(f32), 4, 0)
    j, lane = iota((8, COLS), 0), iota((8, COLS), 1)
    place = jnp.where(lane == jnp.where(j < 4, j, j + COLS - 8), 1.0, 0.0)
    return dot(both, place, 0, 0)


def flux_kernel(q_ref, c_ref, b_ref, a_ref, fe_ref, fw_ref, f_ref, p_ref, w_ref, label_ref, out_ref):
    parts = []
    mine = (q_ref[NA1 - 4 : NA1, :], c_ref[NA1 - 4 : NA1, :], c_ref[2 * NA1 - 4 : 2 * NA1, :])
    nb = b_ref[LOW0:NMSG, :].astype(f32)
    na = a_ref[LOW0:NMSG, :].astype(f32)
    lo_b = beyond(fe_ref[:, NMSG - COLS : NMSG], fw_ref[:, NMSG - COLS : NMSG])[COLS - 16 :]
    o1 = NMSG + NOWN
    lo_o = beyond(fe_ref[:, o1 - COLS : o1], fw_ref[:, o1 - COLS : o1])[COLS - 32 : COLS - 16]
    lo_a = beyond(fe_ref[:, NSTR - COLS :], fw_ref[:, NSTR - COLS :])[COLS - 16 :]
    pad = jnp.zeros((4, COLS), f32)
    for i in range(3):
        s = slice(4 * i, 4 * i + 4)
        main = jnp.concatenate([nb[s], mine[i], na[s], pad], axis=0)
        far = jnp.concatenate([lo_b[s], lo_o[s], lo_a[s], pad], axis=0)
        parts.append(jnp.concatenate([main, far], axis=1))
    q, cx, cy = parts
    xp, xm, yp, ym = jnp.maximum(cx, 0.0), jnp.minimum(cx, 0.0), jnp.maximum(cy, 0.0), jnp.minimum(cy, 0.0)
    aw, xm_w = pltpu.roll(xp, 1, 1), pltpu.roll(xm, 1, 1)
    a_s, ym_s = pltpu.roll(yp, 1, 0), pltpu.roll(ym, 1, 0)
    a0 = 1.0 - xp + xm_w - yp + ym_s
    for _ in range(NSTEP):
        west, east = pltpu.roll(q, 1, 1), pltpu.roll(q, 2 * COLS - 1, 1)
        south, north = pltpu.roll(q, 1, 0), pltpu.roll(q, 15, 0)
        q = (a0 * q + aw * west - xm * east) + (a_s * south - ym * north)
    flux = f_ref[...] * (q[ROWS : 2 * ROWS, :COLS] - p_ref[...])
    flux = jnp.concatenate([flux, jnp.zeros((4, COLS), f32)], axis=0).astype(bf16).astype(f32)
    turned = jnp.concatenate([flux] + [pltpu.roll(flux, SUB * d, 1) for d in range(1, 4)], axis=0).astype(bf16)
    e, k = iota((PADE, 32), 0), iota((PADE, 32), 1)
    turn = (e % 4 - (e // 3) % 4 + 4) % 4
    pick = onehot((e < ENTS) & (k == turn * 8 + e // 12))
    lined = dot(pick, turned, 1, 0)
    e, lane = iota((PADE, COLS), 0), iota((PADE, COLS), 1)
    lined = jnp.where(lane // SUB == e % 4, lined, 0.0)
    spread_flux = jnp.concatenate([jnp.where(e // 4 == j, lined, 0.0) for j in range(ENTS // 4)], axis=1).astype(bf16)
    contrib = dot(spread_flux, w_ref[...], 1, 0).astype(bf16).astype(f32)
    message = jnp.concatenate([contrib[:ENTS], label_ref[...]], axis=0).astype(bf16)
    for i in range(NY):
        out_ref[i * PADE : (i + 1) * PADE, :] = message


def line_up(sums):
    wide = 3 * COLS
    rows = [s[:, r * wide : (r + 1) * wide] for s in sums for r in range(ROWS)]
    stack = jnp.concatenate(rows + [jnp.zeros((8 - len(rows), wide), f32)] * (len(rows) < 8), axis=0)
    src, dst = iota((wide, COLS), 0), iota((wide, COLS), 1)
    move = jnp.where((src % SUB == dst % SUB) & ((src // SUB) // OVL == dst // SUB), 1.0, 0.0)
    return dot(stack, move, 1, 0, precision=lax.Precision.HIGHEST)


def table_kernel(tr_ref, br_ref, w_ref, label_ref, area_ref):
    t = tr_ref[...]
    row = iota((16, COLS), 0)
    z = jnp.where(t < 0, -1, t // NY)
    label = jnp.where(row == 0, z, (t - z * NY) * ROWS + br_ref[...])
    label_ref[...] = jnp.where((row > 1) | (t < 0), -1, label).astype(f32)
    areas = line_up([dot(jnp.ones((16, COLS), bf16), w_ref[...], 1, 1)[0:1]])[0:4]
    area_ref[...] = jnp.concatenate([areas, areas], axis=0)


def gathered_labels(got_ref):
    lane = iota((16, COLS), 1)
    parts = [got_ref[i * PADE + ENTS : (i + 1) * PADE, :].astype(f32) for i in range(NY)]
    pairs = [jnp.where(lane < PADE, parts[i], parts[i + 1]) for i in range(0, NY, 2)]
    both = jnp.concatenate(pairs, axis=1).astype(i32)
    z, yr = both[0:1], both[1:2]
    y = yr // ROWS
    return z, y, yr - y * ROWS


def upright(row):
    n = row.shape[1]
    return jnp.sum(jnp.where(iota((n, n), 0) == iota((n, n), 1), row, 0), axis=1, keepdims=True)


def merge_kernel(ntile, y_ref, got_ref, out_ref):
    me = y_ref[0, 0]
    z, y, r = gathered_labels(got_ref)
    tile = z * NY + y
    n = NY * PADE
    o = iota((8 * ntile // NY, n), 0)
    to, k = (o // 8) * NY + me, o % 8
    after = jnp.where(tile == ntile - 1, 0, tile + 1)
    ahead = jnp.where(tile == 0, ntile - 1, tile - 1)
    real = z >= 0
    own = onehot(real & (tile == to) & (r == k))
    west = onehot(real & (after == to) & (k == 4))
    east = onehot(real & (ahead == to) & (k == 4))
    rcol, lane = upright(r), iota((n, COLS), 1)
    got = got_ref[...].astype(f32)
    west_cells = jnp.where(lane == rcol, got[:, COLS - 1 :], 0.0)
    east_cells = jnp.where(lane == rcol + 4, got[:, :1], 0.0)
    table = jnp.concatenate([got, west_cells, east_cells], axis=0).astype(bf16)
    out_ref[...] = dot(jnp.concatenate([own, west, east], axis=1), table, 1, 0).astype(bf16)


def pick_kernel(ntile, y_ref, got_ref, pick_ref):
    me = y_ref[0, 0]
    z, y, r = gathered_labels(got_ref)
    at = upright(jnp.where((z >= 0) & (y == me), z * 8 + r, -8))
    lane = iota((ENTS, 8 * ntile // NY), 1)
    for i in range(NY):
        for c in range(2):
            start = (2 * i + c) * ENTS
            pick_ref[start : start + ENTS, :] = onehot(lane == at[i * PADE : i * PADE + ENTS] + 4 * c)


def sea_kernel(x_ref, m_ref, b_ref, a_ref, fe_ref, fw_ref, out_ref, wide_ref, x_s, fb_s, fo_s, fa_s):
    o0, o1 = NMSG, NMSG + NOWN
    fb_s[...] = beyond(fe_ref[:, 0:o0], fw_ref[:, 0:o0])
    fo_s[...] = beyond(fe_ref[:, o0:o1], fw_ref[:, o0:o1])
    fa_s[...] = beyond(fe_ref[:, o1:], fw_ref[:, o1:])
    x_s[0 : 2 * NSEA, :] = x_ref[...]
    x_s[2 * NSEA :, :] = jnp.zeros((16, COLS), f32)

    def join(main, far):
        return jnp.concatenate([main, far], axis=1)

    wet = [join(b_ref[WET0 : WET0 + 16, :].astype(f32)[:1], fb_s[WET0 : WET0 + 1, :])]
    mask = m_ref[...].astype(f32)
    for r in range(ROWS):
        wet.append(join(mask[r : r + 1], fo_s[OWET0 + r : OWET0 + r + 1, :]))
    wet.append(join(a_ref[WET0 : WET0 + 16, :].astype(f32)[:1], fa_s[WET0 : WET0 + 1, :]))
    wide_ref[...] = jnp.concatenate(wet + [jnp.zeros((2, 2 * COLS), f32)], axis=0)
    level = iota((OLP, 2 * COLS), 0)
    top, bottom = level == 0, level >= OL - 1

    state = []
    for v in range(2):
        rows = []
        for r in range(2):
            at = SEA0 + (2 * v + r) * OLP
            rows.append(join(b_ref[at : at + OLP, :].astype(f32), fb_s[at : at + OLP, :]))
        for r in range(ROWS):
            at = v * NSEA + r
            rows.append(join(x_s[pl.ds(at, OLP, stride=ROWS), :], fo_s[pl.ds(OSEA0 + at, OLP, stride=ROWS), :]))
        for r in range(2):
            at = SEA0 + (2 * v + r) * OLP
            rows.append(join(a_ref[at : at + OLP, :].astype(f32), fa_s[at : at + OLP, :]))
        state.append(rows)
    for step in range(NOSTEP):
        new = [[], []]
        for j in range(1, len(state[0]) - 1):
            w = wet[j - 1 + step]
            for v in range(2):
                mid = state[v][j]
                ahead, behind = pltpu.roll(mid, 2 * COLS - 1, 1), pltpu.roll(mid, 1, 1)
                lap = state[v][j + 1] + state[v][j - 1] + ahead + behind - 4.0 * mid
                under = jnp.where(bottom, 0.0, pltpu.roll(mid, OLP - 1, 0) - mid)
                over = jnp.where(top, 0.0, mid - pltpu.roll(mid, 1, 0))
                tend = hor_mix * lap + vert_mix * (under - over)
                if v == 0:
                    gradient = ahead - behind
                else:
                    tend = tend - press_grad * gradient
                new[v].append(mid + w * tend)
        state = new
    for v in range(2):
        for r in range(ROWS):
            out_ref[pl.ds(v * NSEA + r, OL, stride=ROWS), :] = state[v][r][:OL, :COLS]


def force_kernel(nz, got_ref, wide_ref, keep_ref, up_ref, down_ref):
    total = jnp.sum(got_ref[...].astype(f32).reshape(nz, 8, COLS), axis=0)
    force, sums = total[0:4], total[4:5]
    r, lane = iota((ROWS, COLS), 0), iota((ROWS, COLS), 1)
    west = jnp.sum(jnp.where(lane == r, sums, 0.0), axis=1, keepdims=True)
    east = jnp.sum(jnp.where(lane == r + 4, sums, 0.0), axis=1, keepdims=True)
    wet = wide_ref[1 : ROWS + 1, :]
    pushed = wet[:, :COLS] * force
    west = wet[:, 2 * COLS - 1 :] * west
    east = wet[:, COLS : COLS + 1] * east
    ahead = jnp.where(lane == COLS - 1, east, pltpu.roll(jnp.concatenate([pushed, pushed], axis=0), COLS - 1, 1)[:ROWS])
    behind = jnp.where(lane == 0, west, pltpu.roll(jnp.concatenate([pushed, pushed], axis=0), 1, 1)[:ROWS])
    keep_ref[...] = jnp.concatenate([pushed, ahead, behind, wet[:, :COLS]], axis=0)
    up_ref[...] = jnp.broadcast_to(pushed[ROWS - 1 :], (8, COLS))
    down_ref[...] = jnp.broadcast_to(pushed[:1], (8, COLS))


def surface_kernel(nz, base_ref, keep_ref, below_ref, above_ref, sent_ref, top_ref):
    pushed, ahead, behind = keep_ref[0:4, :], keep_ref[4:8, :], keep_ref[8:12, :]
    wet = keep_ref[12:16, :]
    upper = jnp.concatenate([pushed[1:], above_ref[0:1, :]], axis=0)
    lower = jnp.concatenate([below_ref[0:1, :], pushed[:-1]], axis=0)
    lap = upper + lower + ahead + behind - 4.0 * pushed
    temp0 = base_ref[0:4, :] + (2.0 * pushed + wet * (hor_mix * lap - vert_mix * pushed))
    temp1 = base_ref[4:8, :] + wet * (vert_mix * pushed)
    cur0 = base_ref[NSEA : NSEA + 4, :] - wet * (press_grad * (ahead - behind))
    top_ref[...] = jnp.concatenate([temp0, temp1, cur0, jnp.zeros((4, COLS), f32)], axis=0)
    surface = jnp.concatenate([temp0, cur0], axis=0)
    sent_ref[...] = jnp.concatenate([surface] * nz, axis=0).astype(bf16)


def air_kernel(q_ref, c_ref, b_ref, a_ref, fe_ref, fw_ref, base_ref, top_ref, air_ref, sea_ref, fb_s, fo_s, fa_s, b_s, a_s):
    sea_ref[...] = base_ref[...]
    sea_ref[0:8, :] = top_ref[0:8, :]
    sea_ref[NSEA : NSEA + 4, :] = top_ref[8:12, :]
    o0, o1 = NMSG, NMSG + NOWN
    fb_s[...] = beyond(fe_ref[:, 0:o0], fw_ref[:, 0:o0])
    fo_s[...] = beyond(fe_ref[:, o0:o1], fw_ref[:, o0:o1])
    fa_s[...] = beyond(fe_ref[:, o1:], fw_ref[:, o1:])
    b_s[...] = b_ref[0:NAIR, :].astype(f32)
    a_s[...] = a_ref[0:NAIR, :].astype(f32)

    def chunk(i, _):
        at = i * 8 * ROWS

        def take(ref, start):
            return ref[pl.ds(start + at, 8, stride=ROWS), :]

        fields = []
        for k in range(3):
            rows = []
            for r in range(ROWS):
                rows.append((take(b_s, k * NA1 + r), take(fb_s, k * NA1 + r)))
            for r in range(ROWS):
                own = take(q_ref, r) if k == 0 else take(c_ref, (k - 1) * NA1 + r)
                rows.append((own, take(fo_s, k * NA1 + r)))
            for r in range(ROWS):
                rows.append((take(a_s, k * NA1 + r), take(fa_s, k * NA1 + r)))
            fields.append([jnp.concatenate(p, axis=1) for p in rows])
        q, cx, cy = fields
        yp, ym = [jnp.maximum(g, 0.0) for g in cy], [jnp.minimum(g, 0.0) for g in cy]
        coefs = [None]
        for j in range(1, 3 * ROWS - 1):
            xp, xm = jnp.maximum(cx[j], 0.0), jnp.minimum(cx[j], 0.0)
            coefs.append((1.0 - xp + pltpu.roll(xm, 1, 1) - yp[j] + ym[j - 1], pltpu.roll(xp, 1, 1), xm))
        for step in range(NSTEP):
            new = []
            for j in range(1, len(q) - 1):
                a0, aw, xm = coefs[step + j]
                west, east = pltpu.roll(q[j], 1, 1), pltpu.roll(q[j], 2 * COLS - 1, 1)
                rest = yp[step + j - 1] * q[j - 1] - ym[step + j] * q[j + 1]
                new.append((a0 * q[j] + aw * west - xm * east) + rest)
            q = new
        for r in range(ROWS):
            air_ref[pl.ds(at + r, 8, stride=ROWS), :] = q[r][:, :COLS]
        return 0

    lax.fori_loop(0, LEV // 8, chunk, 0)


def choose_kernel(came_ref, pick_ref, out_ref):
    out_ref[...] = dot(pick_ref[...], came_ref[...], 1, 0).astype(bf16)


def back_kernel(came_ref, w_ref, area_ref, out_ref):
    n = 2 * ENTS
    values = came_ref[0:n, :].astype(f32)
    for i in range(1, NY):
        values = values + came_ref[i * n : (i + 1) * n, :].astype(f32)
    pairs = dot(values.astype(bf16), w_ref[...], 1, 1)
    e, l = iota((ENTS, SUB * ENTS), 0), iota((ENTS, SUB * ENTS), 1)
    mine = l // SUB == e
    halves = (pairs[:ENTS], pairs[ENTS:])
    sums = [jnp.sum(jnp.where(mine, h, 0.0), axis=0, keepdims=True) for h in halves]
    out_ref[...] = line_up(sums) / area_ref[...]


def body(
    atmosphere_tracer_state,
    courant,
    surface_exchange_factor,
    prior_sea_surface_temper,
    remap_overlay_weight,
    remap_dest_tile,
    remap_dest_block,
    ocean_level_state,
    ocean_cell_mask,
):
    ntile = lax.axis_size("tile")
    sds = jax.ShapeDtypeStruct
    q = atmosphere_tracer_state.reshape(NA1, COLS)
    c = courant.reshape(2 * NA1, COLS)
    x = ocean_level_state.reshape(2 * NSEA, COLS)
    mask = ocean_cell_mask
    weights = remap_overlay_weight.reshape(ENTS * SUB, COLS)
    tiles = jnp.pad(remap_dest_tile[0], (0, PADE - ENTS), constant_values=-1000)
    blocks = jnp.pad(remap_dest_block[0], (0, PADE - ENTS))
    trow, brow = jnp.tile(tiles, 2)[None, :], jnp.tile(blocks, 2)[None, :]
    nz = ntile // NY
    me = jnp.full((1, 1), lax.axis_index("tile") % NY, i32)
    along_y = [[z * NY + y for y in range(NY)] for z in range(nz)]
    along_z = [[z * NY + y for z in range(nz)] for y in range(NY)]

    msg = sds((NMSG, COLS), bf16)
    stay = (lambda a: a) if INTERPRET else (lambda a: pltpu.with_memory_space_constraint(a, pltpu.HBM))
    up, down = call(
        pack_kernel, (msg, msg), *[stay(a) for a in (q, c, x, mask)], far=4,
        scratch=[pltpu.VMEM(a.shape, a.dtype) for a in (q, c, x, mask)] + [pltpu.SemaphoreType.DMA((4,))],
    )
    before = lax.ppermute(up, "comp", ring("comp", 1))
    after = lax.ppermute(down, "comp", ring("comp", -1))
    strip = sds((8, NSTR), bf16)
    west, east = call(strip_kernel, (strip, strip), q, c, x, mask, before, after)
    trow, west, east = lax.optimization_barrier((trow, west, east))
    fe = lax.ppermute(west, "tile", ring("tile", -1))
    fw = lax.ppermute(east, "tile", ring("tile", 1))
    labels, areas = call(table_kernel, (sds((16, COLS), f32), sds((8, COLS), f32)), trow, brow, weights)
    outgoing = call(
        flux_kernel, sds((NY * PADE, COLS), bf16),
        q, c, before, after, fe, fw, surface_exchange_factor, prior_sea_surface_temper, weights, labels,
    )

    def exchange(a, groups):
        n = len(groups[0])
        a = a.reshape(n, -1, COLS)
        a = lax.all_to_all(a, "tile", split_axis=0, concat_axis=0, tiled=True, axis_index_groups=groups)
        return a.reshape(-1, COLS)

    near = exchange(outgoing, along_y)
    merged = call(functools.partial(merge_kernel, ntile), sds((8 * nz, COLS), bf16), me, near, smem=1)
    merged, fe1, near = lax.optimization_barrier((merged, fe, near))
    far = [pltpu.VMEM((n, COLS), f32) for n in (NMSG, NOWN, NMSG)]
    arrived = exchange(merged, along_z)
    picks = call(functools.partial(pick_kernel, ntile), sds((2 * NY * ENTS, 8 * nz), bf16), me, near, smem=1)
    base, wide_wet = call(
        sea_kernel, (sds((2 * NSEA, COLS), f32), sds((8, 2 * COLS), f32)),
        x, mask, before, after, fe1, fw, scratch=[pltpu.VMEM((2 * NSEA + 16, COLS), f32)] + far,
    )
    tile8 = sds((8, COLS), f32)
    keep, to_up, to_down = call(
        functools.partial(force_kernel, nz), (sds((16, COLS), f32), tile8, tile8), arrived, wide_wet
    )
    below = lax.ppermute(to_up, "comp", ring("comp", 1))
    above = lax.ppermute(to_down, "comp", ring("comp", -1))
    sent, top = call(
        functools.partial(surface_kernel, nz), (sds((8 * nz, COLS), bf16), sds((16, COLS), f32)),
        base, keep, below, above,
    )
    sent, top = lax.optimization_barrier((sent, top))
    came = exchange(sent, along_z)
    air_new, ocean_new = call(
        air_kernel, (sds((NA1, COLS), f32), sds((2 * NSEA, COLS), f32)),
        q, c, before, after, fe, fw, base, top, scratch=far + [pltpu.VMEM((NAIR, COLS), f32)] * 2,
    )
    chosen = call(choose_kernel, sds((2 * NY * ENTS, COLS), bf16), came, picks)
    surface_air = call(back_kernel, tile8, exchange(chosen, along_y), weights, areas)
    return (
        air_new.reshape(atmosphere_tracer_state.shape),
        ocean_new.reshape(ocean_level_state.shape),
        surface_air.reshape(2, ROWS, COLS),
    )


def solution(mesh):
    return jax.shard_map(
        body,
        mesh=mesh,
        in_specs=(
            P(None, "comp", "tile"),
            P(None, None, "comp", "tile"),
            P("comp", "tile"),
            P("comp", "tile"),
            P("comp", "tile", None, None),
            P("comp", "tile"),
            P("comp", "tile"),
            P(None, None, "comp", "tile"),
            P("comp", "tile"),
        ),
        out_specs=(P(None, "comp", "tile"), P(None, None, "comp", "tile"), P(None, "comp", "tile")),
        check_vma=False,
    )
```

```python
import functools

import jax
import jax.numpy as jnp
from jax import lax
from jax.experimental import pallas as pl
from jax.experimental.pallas import tpu as pltpu
from jax.sharding import PartitionSpec as P

OVL = 3
NSTEP = 4
NOSTEP = 2
INTERPRET = False

hor_mix = 0.12
vert_mix = 0.2
press_grad = 0.3


bf16 = jnp.bfloat16
f32 = jnp.float32
i32 = jnp.int32

LEV, OL, ROWS, COLS, SUB, ENTS = 72, 62, 4, 128, 32, 48
NAIR = 3 * LEV * ROWS
NA1 = LEV * ROWS
NSEA = OL * ROWS
OLP = 64
SEA0 = NAIR
WET0 = SEA0 + 4 * OLP
FAR0 = WET0 + 16
NMSG = FAR0 + 96
OSEA0 = NAIR
OWET0 = OSEA0 + 2 * NSEA
NOWN = OWET0 + 48
NSTR = NOWN + COLS
PADE = 64


def dot(a, b, ca, cb, **kw):
    return lax.dot_general(a, b, (((ca,), (cb,)), ((), ())), preferred_element_type=f32, **kw)


def iota(shape, axis):
    return lax.broadcasted_iota(i32, shape, axis)


def onehot(mask):
    return jnp.where(mask, 1.0, 0.0).astype(bf16)


def call(kernel, outs, *args, scratch=(), far=0):
    vmem = pl.BlockSpec(memory_space=pltpu.VMEM)
    specs = [pl.BlockSpec(memory_space=pltpu.HBM)] * far + [vmem] * (len(args) - far)
    return pl.pallas_call(
        kernel,
        out_shape=outs,
        in_specs=specs,
        scratch_shapes=list(scratch),
        compiler_params=None if INTERPRET else pltpu.CompilerParams(vmem_limit_bytes=48 << 20),
        interpret=INTERPRET,
    )(*args)


def ring(axis, step):
    size = lax.axis_size(axis)
    return [(i, (i + step) % size) for i in range(size)]


def low_kernel(q_hbm, c_hbm, low_ref, s_ref, sem):
    spots = ((q_hbm, NA1), (c_hbm, NA1), (c_hbm, 2 * NA1))
    copies = [
        pltpu.make_async_copy(src.at[end - 8 : end, :], s_ref.at[8 * i : 8 * i + 8, :], sem.at[i])
        for i, (src, end) in enumerate(spots)
    ]
    for copy in copies:
        copy.start()
    for copy in copies:
        copy.wait()
    pieces = [s_ref[8 * i + 4 : 8 * i + 8, :] for i in range(3)]
    low_ref[...] = jnp.concatenate(pieces + [jnp.zeros((4, COLS), f32)], axis=0).astype(bf16)


def pack_kernel(q_ref, c_ref, x_ref, m_ref, fe_ref, fw_ref, up_ref, down_ref):
    q = q_ref[...].astype(bf16)
    c = c_ref[...].astype(bf16)
    mask = m_ref[...].astype(f32)
    both = fe_ref[:, :NOWN].astype(f32) + pltpu.roll(fw_ref[:, :NOWN].astype(f32), 4, 0)
    blocks = [both[:, j : j + COLS] for j in range(0, NOWN, COLS)]
    far = jnp.concatenate(blocks + [jnp.zeros((8, COLS), f32)], axis=0).astype(bf16)
    for ref, r0, mr in ((up_ref, ROWS - 2, ROWS - 1), (down_ref, 0, 0)):
        ref[0:NA1, :] = q
        ref[NA1:NAIR, :] = c
        for v in range(2):
            for r in range(2):
                at = SEA0 + (2 * v + r) * OLP
                part = x_ref[pl.ds(v * NSEA + r0 + r, OL, stride=ROWS), :]
                ref[at : at + OLP, :] = jnp.concatenate([part, jnp.zeros((OLP - OL, COLS), f32)], axis=0).astype(bf16)
        ref[WET0:FAR0, :] = jnp.broadcast_to(mask[mr : mr + 1], (16, COLS)).astype(bf16)
        ref[FAR0:NMSG, :] = far


def place_matrix(first):
    j, lane = iota((8, COLS), 0), iota((8, COLS), 1)
    return onehot((j < 4) & (lane == (j if first else j + COLS - 4)))


def strip_kernel(q_ref, c_ref, x_ref, m_ref, low_ref, b_ref, a_ref, west_ref, east_ref):
    mask = jnp.concatenate([m_ref[...].astype(f32), jnp.zeros((12, COLS), f32)], axis=0).astype(bf16)
    tail = jnp.concatenate([mask, low_ref[...], jnp.zeros((16, COLS), bf16)], axis=0)
    own = jnp.concatenate([q_ref[...].astype(bf16), c_ref[...].astype(bf16), x_ref[...].astype(bf16), tail], axis=0)
    others = jnp.concatenate([b_ref[...], a_ref[...], jnp.zeros((COLS - 32, COLS), bf16)], axis=0)
    for ref, first in ((west_ref, True), (east_ref, False)):
        place = place_matrix(first)
        ref[:, 0:NOWN] = dot(place, own, 1, 1).astype(bf16)
        ref[:, NOWN:] = dot(place, others, 1, 1).astype(bf16)


def columns(both):
    j, lane = iota((8, COLS), 0), iota((8, COLS), 1)
    place = jnp.where(lane == jnp.where(j < 4, j, j + COLS - 8), 1.0, 0.0)
    return dot(both, place, 0, 0)


def beyond(fe, fw):
    return columns(fe.astype(f32) + pltpu.roll(fw.astype(f32), 4, 0))


def beyond_of(ref):
    far = ref[FAR0:NMSG, :].astype(f32)
    return columns(jnp.concatenate([far[8 * j : 8 * j + 8] for j in range(NOWN // COLS)], axis=1))


def entry_tables(tc_ref, tr_ref):
    tcol = tc_ref[...]
    trow = tr_ref[...]
    e, l = iota((PADE, 4 * PADE), 0), iota((PADE, 4 * PADE), 1)
    same = tcol == trow
    rank_row = jnp.sum(jnp.where(same & (e < l % PADE), 1, 0), axis=0, keepdims=True)
    rank_col = jnp.sum(jnp.where(same & (l < e), 1, 0), axis=1, keepdims=True)
    return tcol, trow, rank_col, rank_row


def flux_kernel(q_ref, c_ref, b_ref, a_ref, fe_ref, fw_ref, f_ref, p_ref, w_ref, spread_ref, mask_ref, out_ref):
    parts = []
    mine = (q_ref[NA1 - 4 : NA1, :], c_ref[NA1 - 4 : NA1, :], c_ref[2 * NA1 - 4 : 2 * NA1, :])
    nb = b_ref[...].astype(f32)
    na = a_ref[...].astype(f32)
    lo = beyond(fe_ref[:, NOWN:], fw_ref[:, NOWN:])
    lo_b, lo_a = lo[0:16], lo[16:32]
    lo_o = beyond(fe_ref[:, NOWN - COLS : NOWN], fw_ref[:, NOWN - COLS : NOWN])[COLS - 32 : COLS - 16]
    pad = jnp.zeros((4, COLS), f32)
    for i in range(3):
        s = slice(4 * i, 4 * i + 4)
        main = jnp.concatenate([nb[s], mine[i], na[s], pad], axis=0)
        far = jnp.concatenate([lo_b[s], lo_o[s], lo_a[s], pad], axis=0)
        parts.append(jnp.concatenate([main, far], axis=1))
    q, cx, cy = parts
    xp, xm, yp, ym = jnp.maximum(cx, 0.0), jnp.minimum(cx, 0.0), jnp.maximum(cy, 0.0), jnp.minimum(cy, 0.0)
    aw, xm_w = pltpu.roll(xp, 1, 1), pltpu.roll(xm, 1, 1)
    a_s, ym_s = pltpu.roll(yp, 1, 0), pltpu.roll(ym, 1, 0)
    a0 = 1.0 - xp + xm_w - yp + ym_s
    for _ in range(NSTEP):
        west, east = pltpu.roll(q, 1, 1), pltpu.roll(q, 2 * COLS - 1, 1)
        south, north = pltpu.roll(q, 1, 0), pltpu.roll(q, 15, 0)
        q = (a0 * q + aw * west - xm * east) + (a_s * south - ym * north)
    flux = f_ref[...] * (q[ROWS : 2 * ROWS, :COLS] - p_ref[...])
    flux = jnp.concatenate([flux, jnp.zeros((4, COLS), f32)], axis=0).astype(bf16).astype(f32)
    turned = jnp.concatenate([flux] + [pltpu.roll(flux, SUB * d, 1) for d in range(1, 4)], axis=0).astype(bf16)
    e, k = iota((PADE, 32), 0), iota((PADE, 32), 1)
    turn = (e % 4 - (e // 3) % 4 + 4) % 4
    pick = onehot((e < ENTS) & (k == turn * 8 + e // 12))
    lined = dot(pick, turned, 1, 0)
    e, lane = iota((PADE, COLS), 0), iota((PADE, COLS), 1)
    lined = jnp.where(lane // SUB == e % 4, lined, 0.0)
    spread_flux = jnp.concatenate([jnp.where(e // 4 == j, lined, 0.0) for j in range(ENTS // 4)], axis=1).astype(bf16)
    contrib = dot(spread_flux, w_ref[...], 1, 0).astype(bf16).astype(f32)
    west = mask_ref[PADE : 2 * PADE, :] * contrib[:, COLS - 1 :]
    east = mask_ref[2 * PADE :, :] * contrib[:, :1]
    table = jnp.concatenate([contrib, mask_ref[0:PADE, :], west, east], axis=0).astype(bf16)
    out_ref[...] = dot(spread_ref[...], table, 1, 0).astype(bf16)


def line_up(sums):
    wide = 3 * COLS
    rows = [s[:, r * wide : (r + 1) * wide] for s in sums for r in range(ROWS)]
    stack = jnp.concatenate(rows + [jnp.zeros((8 - len(rows), wide), f32)] * (len(rows) < 8), axis=0)
    src, dst = iota((wide, COLS), 0), iota((wide, COLS), 1)
    move = jnp.where((src % SUB == dst % SUB) & ((src // SUB) // OVL == dst // SUB), 1.0, 0.0)
    return dot(stack, move, 1, 0, precision=lax.Precision.HIGHEST)


def table_kernel(ntile, tc_ref, tr_ref, bc_ref, w_ref, spread_ref, mask_ref, want_ref, area_ref):
    tcol, trow, rank_col, rank_row = entry_tables(tc_ref, tr_ref)
    lane = iota((PADE, COLS), 1)
    hit = (lane % 4 == bc_ref[...]) & ((lane // 4) % 2 == rank_col)
    spans = ((0, 16), (16, 24), (24, 32))
    mask_ref[...] = jnp.concatenate([jnp.where(hit & (lane >= a) & (lane < b), 1.0, 0.0) for a, b in spans], axis=0)
    kind = iota((1, 4 * PADE), 1) // PADE
    to = jnp.where(kind == 2, jnp.where(trow == ntile - 1, 0, trow + 1), trow)
    to = jnp.where(kind == 3, jnp.where(trow == 0, ntile - 1, trow - 1), to)
    slot = jnp.where(kind == 0, rank_row, 2)
    spread_ref[...] = onehot(iota((4 * ntile, 4 * PADE), 0) == to * 4 + slot)
    at = tcol * 4 + rank_col * 2
    col = iota((PADE, 4 * ntile), 1)
    want_ref[...] = jnp.concatenate([onehot(col == at), onehot(col == at + 1)], axis=0)
    areas = line_up([dot(jnp.ones((16, COLS), bf16), w_ref[...], 1, 1)[0:1]])[0:4]
    area_ref[...] = jnp.concatenate([areas, areas], axis=0)


def sea_kernel(x_ref, m_ref, b_ref, a_ref, fe_ref, fw_ref, out_ref, wide_ref, x_s, fb_s, fo_s, fa_s):
    fb_s[...] = beyond_of(b_ref)
    fo_s[...] = beyond(fe_ref[:, :NOWN], fw_ref[:, :NOWN])
    fa_s[...] = beyond_of(a_ref)
    x_s[0 : 2 * NSEA, :] = x_ref[...]
    x_s[2 * NSEA :, :] = jnp.zeros((16, COLS), f32)

    def join(main, far):
        return jnp.concatenate([main, far], axis=1)

    wet = [join(b_ref[WET0 : WET0 + 16, :].astype(f32)[:1], fb_s[OWET0 + ROWS - 1 : OWET0 + ROWS, :])]
    mask = m_ref[...].astype(f32)
    for r in range(ROWS):
        wet.append(join(mask[r : r + 1], fo_s[OWET0 + r : OWET0 + r + 1, :]))
    wet.append(join(a_ref[WET0 : WET0 + 16, :].astype(f32)[:1], fa_s[OWET0 : OWET0 + 1, :]))
    wide_ref[...] = jnp.concatenate(wet + [jnp.zeros((2, 2 * COLS), f32)], axis=0)
    level = iota((OLP, 2 * COLS), 0)
    top, bottom = level == 0, level >= OL - 1

    state = []
    for v in range(2):
        rows = []
        for r in range(2):
            at = SEA0 + (2 * v + r) * OLP
            far = fb_s[pl.ds(OSEA0 + v * NSEA + ROWS - 2 + r, OLP, stride=ROWS), :]
            rows.append(join(b_ref[at : at + OLP, :].astype(f32), far))
        for r in range(ROWS):
            at = v * NSEA + r
            rows.append(join(x_s[pl.ds(at, OLP, stride=ROWS), :], fo_s[pl.ds(OSEA0 + at, OLP, stride=ROWS), :]))
        for r in range(2):
            at = SEA0 + (2 * v + r) * OLP
            far = fa_s[pl.ds(OSEA0 + v * NSEA + r, OLP, stride=ROWS), :]
            rows.append(join(a_ref[at : at + OLP, :].astype(f32), far))
        state.append(rows)
    for step in range(NOSTEP):
        new = [[], []]
        for j in range(1, len(state[0]) - 1):
            w = wet[j - 1 + step]
            for v in range(2):
                mid = state[v][j]
                ahead, behind = pltpu.roll(mid, 2 * COLS - 1, 1), pltpu.roll(mid, 1, 1)
                lap = state[v][j + 1] + state[v][j - 1] + ahead + behind - 4.0 * mid
                under = jnp.where(bottom, 0.0, pltpu.roll(mid, OLP - 1, 0) - mid)
                over = jnp.where(top, 0.0, mid - pltpu.roll(mid, 1, 0))
                tend = hor_mix * lap + vert_mix * (under - over)
                if v == 0:
                    gradient = ahead - behind
                else:
                    tend = tend - press_grad * gradient
                new[v].append(mid + w * tend)
        state = new
    for v in range(2):
        for r in range(ROWS):
            out_ref[pl.ds(v * NSEA + r, OL, stride=ROWS), :] = state[v][r][:OL, :COLS]


def force_kernel(ntile, got_ref, wide_ref, aux_ref, keep_ref, up_ref, down_ref, s_ref):
    s_ref[...] = got_ref[...].astype(f32)
    first = s_ref[pl.ds(0, ntile, stride=4), :].astype(bf16)
    second = s_ref[pl.ds(1, ntile, stride=4), :].astype(bf16)
    aux32 = s_ref[pl.ds(2, ntile, stride=4), :]
    aux = aux32.astype(bf16)
    aux_ref[...] = aux
    force = dot(aux32, first.astype(f32), 0, 0)[0:4] + dot(aux32, second.astype(f32), 0, 0)[4:8]
    sums = jnp.sum(aux32, axis=0, keepdims=True)
    r, lane = iota((ROWS, COLS), 0), iota((ROWS, COLS), 1)
    mine = lane % 4 == r
    west = jnp.sum(jnp.where(mine & (lane >= 16) & (lane < 24), sums, 0.0), axis=1, keepdims=True)
    east = jnp.sum(jnp.where(mine & (lane >= 24) & (lane < 32), sums, 0.0), axis=1, keepdims=True)
    wet = wide_ref[1 : ROWS + 1, :]
    pushed = wet[:, :COLS] * force
    west = wet[:, 2 * COLS - 1 :] * west
    east = wet[:, COLS : COLS + 1] * east
    ahead = jnp.where(lane == COLS - 1, east, pltpu.roll(jnp.concatenate([pushed, pushed], axis=0), COLS - 1, 1)[:ROWS])
    behind = jnp.where(lane == 0, west, pltpu.roll(jnp.concatenate([pushed, pushed], axis=0), 1, 1)[:ROWS])
    keep_ref[...] = jnp.concatenate([pushed, ahead, behind, wet[:, :COLS]], axis=0)
    up_ref[...] = jnp.broadcast_to(pushed[ROWS - 1 :], (8, COLS))
    down_ref[...] = jnp.broadcast_to(pushed[:1], (8, COLS))


def surface_kernel(ntile, base_ref, keep_ref, below_ref, above_ref, aux_ref, sent_ref, top_ref, s_ref):
    pushed, ahead, behind = keep_ref[0:4, :], keep_ref[4:8, :], keep_ref[8:12, :]
    wet = keep_ref[12:16, :]
    upper = jnp.concatenate([pushed[1:], above_ref[0:1, :]], axis=0)
    lower = jnp.concatenate([below_ref[0:1, :], pushed[:-1]], axis=0)
    lap = upper + lower + ahead + behind - 4.0 * pushed
    temp0 = base_ref[0:4, :] + (2.0 * pushed + wet * (hor_mix * lap - vert_mix * pushed))
    temp1 = base_ref[4:8, :] + wet * (vert_mix * pushed)
    cur0 = base_ref[NSEA : NSEA + 4, :] - wet * (press_grad * (ahead - behind))
    top_ref[...] = jnp.concatenate([temp0, temp1, cur0, jnp.zeros((4, COLS), f32)], axis=0)
    table = jnp.concatenate([temp0, temp0, cur0, cur0], axis=0)
    row = iota((16, COLS), 0)
    aux = aux_ref[...][:, :16]
    for slot in range(2):
        for c in range(2):
            part = jnp.where(row // 4 == 2 * c + slot, table, 0.0).astype(bf16)
            s_ref[pl.ds(2 * slot + c, ntile, stride=4), :] = dot(aux, part, 1, 0)
    sent_ref[...] = s_ref[...].astype(bf16)


def air_kernel(q_ref, c_ref, b_ref, a_ref, fe_ref, fw_ref, base_ref, top_ref, air_ref, sea_ref, fb_s, fo_s, fa_s, b_s, a_s):
    sea_ref[...] = base_ref[...]
    sea_ref[0:8, :] = top_ref[0:8, :]
    sea_ref[NSEA : NSEA + 4, :] = top_ref[8:12, :]
    fb_s[...] = beyond_of(b_ref)
    fo_s[...] = beyond(fe_ref[:, :NOWN], fw_ref[:, :NOWN])
    fa_s[...] = beyond_of(a_ref)
    b_s[...] = b_ref[0:NAIR, :].astype(f32)
    a_s[...] = a_ref[0:NAIR, :].astype(f32)

    def chunk(i, _):
        at = i * 8 * ROWS

        def take(ref, start):
            return ref[pl.ds(start + at, 8, stride=ROWS), :]

        fields = []
        for k in range(3):
            rows = []
            for r in range(ROWS):
                rows.append((take(b_s, k * NA1 + r), take(fb_s, k * NA1 + r)))
            for r in range(ROWS):
                own = take(q_ref, r) if k == 0 else take(c_ref, (k - 1) * NA1 + r)
                rows.append((own, take(fo_s, k * NA1 + r)))
            for r in range(ROWS):
                rows.append((take(a_s, k * NA1 + r), take(fa_s, k * NA1 + r)))
            fields.append([jnp.concatenate(p, axis=1) for p in rows])
        q, cx, cy = fields
        yp, ym = [jnp.maximum(g, 0.0) for g in cy], [jnp.minimum(g, 0.0) for g in cy]
        coefs = [None]
        for j in range(1, 3 * ROWS - 1):
            xp, xm = jnp.maximum(cx[j], 0.0), jnp.minimum(cx[j], 0.0)
            coefs.append((1.0 - xp + pltpu.roll(xm, 1, 1) - yp[j] + ym[j - 1], pltpu.roll(xp, 1, 1), xm))
        for step in range(NSTEP):
            new = []
            for j in range(1, len(q) - 1):
                a0, aw, xm = coefs[step + j]
                west, east = pltpu.roll(q[j], 1, 1), pltpu.roll(q[j], 2 * COLS - 1, 1)
                rest = yp[step + j - 1] * q[j - 1] - ym[step + j] * q[j + 1]
                new.append((a0 * q[j] + aw * west - xm * east) + rest)
            q = new
        for r in range(ROWS):
            air_ref[pl.ds(at + r, 8, stride=ROWS), :] = q[r][:, :COLS]
        return 0

    lax.fori_loop(0, LEV // 8, chunk, 0)


def back_kernel(came_ref, w_ref, want_ref, area_ref, out_ref):
    values = dot(want_ref[...], came_ref[...], 1, 0).astype(bf16)
    pairs = dot(values, w_ref[...], 1, 1)
    e, l = iota((PADE, SUB * ENTS), 0), iota((PADE, SUB * ENTS), 1)
    mine = l // SUB == e
    halves = (pairs[:PADE], pairs[PADE:])
    sums = [jnp.sum(jnp.where(mine, h, 0.0), axis=0, keepdims=True) for h in halves]
    out_ref[...] = line_up(sums) / area_ref[...]


def body(
    atmosphere_tracer_state,
    courant,
    surface_exchange_factor,
    prior_sea_surface_temper,
    remap_overlay_weight,
    remap_dest_tile,
    remap_dest_block,
    ocean_level_state,
    ocean_cell_mask,
):
    ntile = lax.axis_size("tile")
    sds = jax.ShapeDtypeStruct
    q = atmosphere_tracer_state.reshape(NA1, COLS)
    c = courant.reshape(2 * NA1, COLS)
    x = ocean_level_state.reshape(2 * NSEA, COLS)
    mask = ocean_cell_mask
    weights = remap_overlay_weight.reshape(ENTS * SUB, COLS)
    tiles = jnp.pad(remap_dest_tile[0], (0, PADE - ENTS), constant_values=-1000)
    blocks = jnp.pad(remap_dest_block[0], (0, PADE - ENTS))
    tcol, bcol = tiles[:, None], blocks[:, None]
    trow = jnp.tile(tiles, 4)[None, :]

    stay = (lambda a: a) if INTERPRET else (lambda a: pltpu.with_memory_space_constraint(a, pltpu.HBM))
    low = call(
        low_kernel, sds((16, COLS), bf16), stay(q), stay(c), far=2,
        scratch=[pltpu.VMEM((24, COLS), f32), pltpu.SemaphoreType.DMA((3,))],
    )
    low_b = lax.ppermute(low, "comp", ring("comp", 1))
    low_a = lax.ppermute(low, "comp", ring("comp", -1))
    strip = sds((8, NSTR), bf16)
    west, east = call(strip_kernel, (strip, strip), q, c, x, mask, low, low_b, low_a)
    slots = sds((4 * ntile, COLS), bf16)
    tcol, west, east = lax.optimization_barrier((tcol, west, east))
    fe = lax.ppermute(west, "tile", ring("tile", -1))
    fw = lax.ppermute(east, "tile", ring("tile", 1))
    spread, masks, want, areas = call(
        functools.partial(table_kernel, ntile),
        (sds((4 * ntile, 4 * PADE), bf16), sds((3 * PADE, COLS), f32), sds((2 * PADE, 4 * ntile), bf16), sds((8, COLS), f32)),
        tcol, trow, bcol, weights,
    )
    outgoing = call(
        flux_kernel, slots,
        q, c, low_b, low_a, fe, fw, surface_exchange_factor, prior_sea_surface_temper, weights, spread, masks,
    )
    outgoing, fe1 = lax.optimization_barrier((outgoing, fe))

    def exchange(a):
        a = a.reshape(ntile, 4, COLS)
        return lax.all_to_all(a, "tile", split_axis=0, concat_axis=0, tiled=True).reshape(4 * ntile, COLS)

    far = [pltpu.VMEM((NOWN, COLS), f32)] * 3
    arrived = exchange(outgoing)
    msg = sds((NMSG, COLS), bf16)
    up, down = call(pack_kernel, (msg, msg), q, c, x, mask, fe1, fw)
    before = lax.ppermute(up, "comp", ring("comp", 1))
    after = lax.ppermute(down, "comp", ring("comp", -1))
    base, wide_wet = call(
        sea_kernel, (sds((2 * NSEA, COLS), f32), sds((8, 2 * COLS), f32)),
        x, mask, before, after, fe1, fw, scratch=[pltpu.VMEM((2 * NSEA + 16, COLS), f32)] + far,
    )
    tile8 = sds((8, COLS), f32)
    aux, keep, to_up, to_down = call(
        functools.partial(force_kernel, ntile), (sds((ntile, COLS), bf16), sds((16, COLS), f32), tile8, tile8),
        arrived, wide_wet, scratch=[pltpu.VMEM((4 * ntile, COLS), f32)],
    )
    below = lax.ppermute(to_up, "comp", ring("comp", 1))
    above = lax.ppermute(to_down, "comp", ring("comp", -1))
    sent, top = call(
        functools.partial(surface_kernel, ntile), (slots, sds((16, COLS), f32)),
        base, keep, below, above, aux, scratch=[pltpu.VMEM((4 * ntile, COLS), f32)],
    )
    sent, top = lax.optimization_barrier((sent, top))
    came = exchange(sent)
    air_new, ocean_new = call(
        air_kernel, (sds((NA1, COLS), f32), sds((2 * NSEA, COLS), f32)),
        q, c, before, after, fe, fw, base, top, scratch=far + [pltpu.VMEM((NAIR, COLS), f32)] * 2,
    )
    surface_air = call(back_kernel, tile8, came, weights, want, areas)
    return (
        air_new.reshape(atmosphere_tracer_state.shape),
        ocean_new.reshape(ocean_level_state.shape),
        surface_air.reshape(2, ROWS, COLS),
    )


def solution(mesh):
    return jax.shard_map(
        body,
        mesh=mesh,
        in_specs=(
            P(None, "comp", "tile"),
            P(None, None, "comp", "tile"),
            P("comp", "tile"),
            P("comp", "tile"),
            P("comp", "tile", None, None),
            P("comp", "tile"),
            P("comp", "tile"),
            P(None, None, "comp", "tile"),
            P("comp", "tile"),
        ),
        out_specs=(P(None, "comp", "tile"), P(None, None, "comp", "tile"), P(None, "comp", "tile")),
        check_vma=False,
    )
```

```python
import functools

import jax
import jax.numpy as jnp
from jax import lax
from jax.experimental import pallas as pl
from jax.experimental.pallas import tpu as pltpu
from jax.sharding import PartitionSpec as P

OVL = 3
NSTEP = 4
NOSTEP = 2
INTERPRET = False

hor_mix = 0.12
vert_mix = 0.2
press_grad = 0.3


bf16 = jnp.bfloat16
f32 = jnp.float32
i32 = jnp.int32

LEV, OL, ROWS, COLS, SUB, ENTS = 72, 62, 4, 128, 32, 48
NAIR = 3 * LEV * ROWS
NA1 = LEV * ROWS
NSEA = OL * ROWS
OLP = 64
SEA0 = NAIR
WET0 = SEA0 + 4 * OLP
FAR0 = WET0 + 16
NMSG = FAR0 + 96
OSEA0 = NAIR
OWET0 = OSEA0 + 2 * NSEA
NOWN = OWET0 + 48
NSTR = NOWN + COLS
PADE = 64


def dot(a, b, ca, cb, **kw):
    return lax.dot_general(a, b, (((ca,), (cb,)), ((), ())), preferred_element_type=f32, **kw)


def iota(shape, axis):
    return lax.broadcasted_iota(i32, shape, axis)


def onehot(mask):
    return jnp.where(mask, 1.0, 0.0).astype(bf16)


def call(kernel, outs, *args, scratch=(), far=0):
    vmem = pl.BlockSpec(memory_space=pltpu.VMEM)
    specs = [pl.BlockSpec(memory_space=pltpu.HBM)] * far + [vmem] * (len(args) - far)
    return pl.pallas_call(
        kernel,
        out_shape=outs,
        in_specs=specs,
        scratch_shapes=list(scratch),
        compiler_params=None if INTERPRET else pltpu.CompilerParams(vmem_limit_bytes=48 << 20),
        interpret=INTERPRET,
    )(*args)


def ring(axis, step):
    size = lax.axis_size(axis)
    return [(i, (i + step) % size) for i in range(size)]


def low_kernel(q_hbm, c_hbm, x_hbm, low_ref, x_ref, s_ref, sem):
    spots = ((q_hbm, NA1), (c_hbm, NA1), (c_hbm, 2 * NA1))
    copies = [
        pltpu.make_async_copy(src.at[end - 8 : end, :], s_ref.at[8 * i : 8 * i + 8, :], sem.at[i])
        for i, (src, end) in enumerate(spots)
    ]
    copies.append(pltpu.make_async_copy(x_hbm, x_ref, sem.at[3]))
    for copy in copies:
        copy.start()
    for copy in copies:
        copy.wait()
    pieces = [s_ref[8 * i + 4 : 8 * i + 8, :] for i in range(3)]
    low_ref[...] = jnp.concatenate(pieces + [jnp.zeros((4, COLS), f32)], axis=0).astype(bf16)


def pack_kernel(q_ref, c_ref, x_ref, m_ref, fe_ref, fw_ref, up_ref, down_ref):
    q = q_ref[...].astype(bf16)
    c = c_ref[...].astype(bf16)
    mask = m_ref[...].astype(f32)
    both = fe_ref[:, :NOWN].astype(f32) + pltpu.roll(fw_ref[:, :NOWN].astype(f32), 4, 0)
    blocks = [both[:, j : j + COLS] for j in range(0, NOWN, COLS)]
    far = jnp.concatenate(blocks + [jnp.zeros((8, COLS), f32)], axis=0).astype(bf16)
    for ref, r0, mr in ((up_ref, ROWS - 2, ROWS - 1), (down_ref, 0, 0)):
        ref[0:NA1, :] = q
        ref[NA1:NAIR, :] = c
        for v in range(2):
            for r in range(2):
                at = SEA0 + (2 * v + r) * OLP
                part = x_ref[pl.ds(v * NSEA + r0 + r, OL, stride=ROWS), :]
                ref[at : at + OLP, :] = jnp.concatenate([part, jnp.zeros((OLP - OL, COLS), f32)], axis=0).astype(bf16)
        ref[WET0:FAR0, :] = jnp.broadcast_to(mask[mr : mr + 1], (16, COLS)).astype(bf16)
        ref[FAR0:NMSG, :] = far


def place_matrix(first):
    j, lane = iota((8, COLS), 0), iota((8, COLS), 1)
    return onehot((j < 4) & (lane == (j if first else j + COLS - 4)))


def strip_kernel(q_ref, c_ref, x_ref, m_ref, low_ref, b_ref, a_ref, west_ref, east_ref):
    mask = jnp.concatenate([m_ref[...].astype(f32), jnp.zeros((12, COLS), f32)], axis=0).astype(bf16)
    tail = jnp.concatenate([mask, low_ref[...], jnp.zeros((16, COLS), bf16)], axis=0)
    own = jnp.concatenate([q_ref[...].astype(bf16), c_ref[...].astype(bf16), x_ref[...].astype(bf16), tail], axis=0)
    others = jnp.concatenate([b_ref[...], a_ref[...], jnp.zeros((COLS - 32, COLS), bf16)], axis=0)
    for ref, first in ((west_ref, True), (east_ref, False)):
        place = place_matrix(first)
        ref[:, 0:NOWN] = dot(place, own, 1, 1).astype(bf16)
        ref[:, NOWN:] = dot(place, others, 1, 1).astype(bf16)


def columns(both):
    j, lane = iota((8, COLS), 0), iota((8, COLS), 1)
    place = jnp.where(lane == jnp.where(j < 4, j, j + COLS - 8), 1.0, 0.0)
    return dot(both, place, 0, 0)


def beyond(fe, fw):
    return columns(fe.astype(f32) + pltpu.roll(fw.astype(f32), 4, 0))


def beyond_of(ref):
    far = ref[FAR0:NMSG, :].astype(f32)
    return columns(jnp.concatenate([far[8 * j : 8 * j + 8] for j in range(NOWN // COLS)], axis=1))


def entry_tables(tc_ref, tr_ref):
    tcol = tc_ref[...]
    trow = tr_ref[...]
    e, l = iota((PADE, 4 * PADE), 0), iota((PADE, 4 * PADE), 1)
    same = tcol == trow
    rank_row = jnp.sum(jnp.where(same & (e < l % PADE), 1, 0), axis=0, keepdims=True)
    rank_col = jnp.sum(jnp.where(same & (l < e), 1, 0), axis=1, keepdims=True)
    return tcol, trow, rank_col, rank_row


def flux_kernel(q_ref, c_ref, b_ref, a_ref, fe_ref, fw_ref, f_ref, p_ref, w_ref, spread_ref, mask_ref, out_ref):
    parts = []
    mine = (q_ref[NA1 - 4 : NA1, :], c_ref[NA1 - 4 : NA1, :], c_ref[2 * NA1 - 4 : 2 * NA1, :])
    nb = b_ref[...].astype(f32)
    na = a_ref[...].astype(f32)
    lo = beyond(fe_ref[:, NOWN:], fw_ref[:, NOWN:])
    lo_b, lo_a = lo[0:16], lo[16:32]
    lo_o = beyond(fe_ref[:, NOWN - COLS : NOWN], fw_ref[:, NOWN - COLS : NOWN])[COLS - 32 : COLS - 16]
    pad = jnp.zeros((4, COLS), f32)
    for i in range(3):
        s = slice(4 * i, 4 * i + 4)
        main = jnp.concatenate([nb[s], mine[i], na[s], pad], axis=0)
        far = jnp.concatenate([lo_b[s], lo_o[s], lo_a[s], pad], axis=0)
        parts.append(jnp.concatenate([main, far], axis=1))
    q, cx, cy = parts
    xp, xm, yp, ym = jnp.maximum(cx, 0.0), jnp.minimum(cx, 0.0), jnp.maximum(cy, 0.0), jnp.minimum(cy, 0.0)
    aw, xm_w = pltpu.roll(xp, 1, 1), pltpu.roll(xm, 1, 1)
    a_s, ym_s = pltpu.roll(yp, 1, 0), pltpu.roll(ym, 1, 0)
    a0 = 1.0 - xp + xm_w - yp + ym_s
    for _ in range(NSTEP):
        west, east = pltpu.roll(q, 1, 1), pltpu.roll(q, 2 * COLS - 1, 1)
        south, north = pltpu.roll(q, 1, 0), pltpu.roll(q, 15, 0)
        q = (a0 * q + aw * west - xm * east) + (a_s * south - ym * north)
    flux = f_ref[...] * (q[ROWS : 2 * ROWS, :COLS] - p_ref[...])
    flux = jnp.concatenate([flux, jnp.zeros((4, COLS), f32)], axis=0).astype(bf16).astype(f32)
    turned = jnp.concatenate([flux] + [pltpu.roll(flux, SUB * d, 1) for d in range(1, 4)], axis=0).astype(bf16)
    e, k = iota((PADE, 32), 0), iota((PADE, 32), 1)
    turn = (e % 4 - (e // 3) % 4 + 4) % 4
    pick = onehot((e < ENTS) & (k == turn * 8 + e // 12))
    lined = dot(pick, turned, 1, 0)
    e, lane = iota((PADE, COLS), 0), iota((PADE, COLS), 1)
    lined = jnp.where(lane // SUB == e % 4, lined, 0.0)
    spread_flux = jnp.concatenate([jnp.where(e // 4 == j, lined, 0.0) for j in range(ENTS // 4)], axis=1).astype(bf16)
    contrib = dot(spread_flux, w_ref[...], 1, 0).astype(bf16).astype(f32)
    west = mask_ref[PADE : 2 * PADE, :] * contrib[:, COLS - 1 :]
    east = mask_ref[2 * PADE :, :] * contrib[:, :1]
    table = jnp.concatenate([contrib, mask_ref[0:PADE, :], west, east], axis=0).astype(bf16)
    out_ref[...] = dot(spread_ref[...], table, 1, 0).astype(bf16)


def line_up(sums):
    wide = 3 * COLS
    rows = [s[:, r * wide : (r + 1) * wide] for s in sums for r in range(ROWS)]
    stack = jnp.concatenate(rows + [jnp.zeros((8 - len(rows), wide), f32)] * (len(rows) < 8), axis=0)
    src, dst = iota((wide, COLS), 0), iota((wide, COLS), 1)
    move = onehot((src % SUB == dst % SUB) & ((src // SUB) // OVL == dst // SUB))
    high = stack.astype(bf16)
    both = dot(jnp.concatenate([high, (stack - high.astype(f32)).astype(bf16)], axis=0), move, 1, 0)
    return both[:8] + both[8:]


def table_kernel(ntile, tc_ref, tr_ref, bc_ref, w_ref, spread_ref, mask_ref, want_ref, area_ref):
    tcol, trow, rank_col, rank_row = entry_tables(tc_ref, tr_ref)
    lane = iota((PADE, COLS), 1)
    hit = (lane % 4 == bc_ref[...]) & ((lane // 4) % 2 == rank_col)
    spans = ((0, 16), (16, 24), (24, 32))
    mask_ref[...] = jnp.concatenate([jnp.where(hit & (lane >= a) & (lane < b), 1.0, 0.0) for a, b in spans], axis=0)
    kind = iota((1, 4 * PADE), 1) // PADE
    to = jnp.where(kind == 2, jnp.where(trow == ntile - 1, 0, trow + 1), trow)
    to = jnp.where(kind == 3, jnp.where(trow == 0, ntile - 1, trow - 1), to)
    slot = jnp.where(kind == 0, rank_row, 2)
    spread_ref[...] = onehot(iota((4 * ntile, 4 * PADE), 0) == to * 4 + slot)
    at = tcol * 4 + rank_col * 2
    col = iota((PADE, 4 * ntile), 1)
    want_ref[...] = jnp.concatenate([onehot(col == at), onehot(col == at + 1)], axis=0)
    areas = line_up([dot(jnp.ones((16, COLS), bf16), w_ref[...], 1, 1)[0:1]])[0:4]
    area_ref[...] = jnp.concatenate([areas, areas], axis=0)


def sea_kernel(x_ref, m_ref, b_ref, a_ref, fe_ref, fw_ref, out_ref, wide_ref, x_s, fb_s, fo_s, fa_s):
    fb_s[...] = beyond_of(b_ref)
    fo_s[...] = beyond(fe_ref[:, :NOWN], fw_ref[:, :NOWN])
    fa_s[...] = beyond_of(a_ref)
    x_s[0 : 2 * NSEA, :] = x_ref[...]
    x_s[2 * NSEA :, :] = jnp.zeros((16, COLS), f32)

    def join(main, far):
        return jnp.concatenate([main, far], axis=1)

    wet = [join(b_ref[WET0 : WET0 + 16, :].astype(f32)[:1], fb_s[OWET0 + ROWS - 1 : OWET0 + ROWS, :])]
    mask = m_ref[...].astype(f32)
    for r in range(ROWS):
        wet.append(join(mask[r : r + 1], fo_s[OWET0 + r : OWET0 + r + 1, :]))
    wet.append(join(a_ref[WET0 : WET0 + 16, :].astype(f32)[:1], fa_s[OWET0 : OWET0 + 1, :]))
    wide_ref[...] = jnp.concatenate(wet + [jnp.zeros((2, 2 * COLS), f32)], axis=0)
    level = iota((OLP, 2 * COLS), 0)
    top, bottom = level == 0, level >= OL - 1

    state = []
    for v in range(2):
        rows = []
        for r in range(2):
            at = SEA0 + (2 * v + r) * OLP
            far = fb_s[pl.ds(OSEA0 + v * NSEA + ROWS - 2 + r, OLP, stride=ROWS), :]
            rows.append(join(b_ref[at : at + OLP, :].astype(f32), far))
        for r in range(ROWS):
            at = v * NSEA + r
            rows.append(join(x_s[pl.ds(at, OLP, stride=ROWS), :], fo_s[pl.ds(OSEA0 + at, OLP, stride=ROWS), :]))
        for r in range(2):
            at = SEA0 + (2 * v + r) * OLP
            far = fa_s[pl.ds(OSEA0 + v * NSEA + r, OLP, stride=ROWS), :]
            rows.append(join(a_ref[at : at + OLP, :].astype(f32), far))
        state.append(rows)
    for step in range(NOSTEP):
        new = [[], []]
        for j in range(1, len(state[0]) - 1):
            w = wet[j - 1 + step]
            for v in range(2):
                mid = state[v][j]
                ahead, behind = pltpu.roll(mid, 2 * COLS - 1, 1), pltpu.roll(mid, 1, 1)
                lap = state[v][j + 1] + state[v][j - 1] + ahead + behind - 4.0 * mid
                under = jnp.where(bottom, 0.0, pltpu.roll(mid, OLP - 1, 0) - mid)
                over = jnp.where(top, 0.0, mid - pltpu.roll(mid, 1, 0))
                tend = hor_mix * lap + vert_mix * (under - over)
                if v == 0:
                    gradient = ahead - behind
                else:
                    tend = tend - press_grad * gradient
                new[v].append(mid + w * tend)
        state = new
    for v in range(2):
        for r in range(ROWS):
            out_ref[pl.ds(v * NSEA + r, OL, stride=ROWS), :] = state[v][r][:OL, :COLS]


def force_kernel(ntile, got_ref, wide_ref, aux_ref, keep_ref, up_ref, down_ref, s_ref):
    s_ref[...] = got_ref[...].astype(f32)
    first = s_ref[pl.ds(0, ntile, stride=4), :].astype(bf16)
    second = s_ref[pl.ds(1, ntile, stride=4), :].astype(bf16)
    aux32 = s_ref[pl.ds(2, ntile, stride=4), :]
    aux = aux32.astype(bf16)
    aux_ref[...] = aux
    force = dot(aux32, first.astype(f32), 0, 0)[0:4] + dot(aux32, second.astype(f32), 0, 0)[4:8]
    sums = jnp.sum(aux32, axis=0, keepdims=True)
    r, lane = iota((ROWS, COLS), 0), iota((ROWS, COLS), 1)
    mine = lane % 4 == r
    west = jnp.sum(jnp.where(mine & (lane >= 16) & (lane < 24), sums, 0.0), axis=1, keepdims=True)
    east = jnp.sum(jnp.where(mine & (lane >= 24) & (lane < 32), sums, 0.0), axis=1, keepdims=True)
    wet = wide_ref[1 : ROWS + 1, :]
    pushed = wet[:, :COLS] * force
    west = wet[:, 2 * COLS - 1 :] * west
    east = wet[:, COLS : COLS + 1] * east
    ahead = jnp.where(lane == COLS - 1, east, pltpu.roll(jnp.concatenate([pushed, pushed], axis=0), COLS - 1, 1)[:ROWS])
    behind = jnp.where(lane == 0, west, pltpu.roll(jnp.concatenate([pushed, pushed], axis=0), 1, 1)[:ROWS])
    keep_ref[...] = jnp.concatenate([pushed, ahead, behind, wet[:, :COLS]], axis=0)
    up_ref[...] = jnp.broadcast_to(pushed[ROWS - 1 :], (8, COLS))
    down_ref[...] = jnp.broadcast_to(pushed[:1], (8, COLS))


def surface_kernel(ntile, base_ref, keep_ref, below_ref, above_ref, aux_ref, sent_ref, top_ref, s_ref):
    pushed, ahead, behind = keep_ref[0:4, :], keep_ref[4:8, :], keep_ref[8:12, :]
    wet = keep_ref[12:16, :]
    upper = jnp.concatenate([pushed[1:], above_ref[0:1, :]], axis=0)
    lower = jnp.concatenate([below_ref[0:1, :], pushed[:-1]], axis=0)
    lap = upper + lower + ahead + behind - 4.0 * pushed
    temp0 = base_ref[0:4, :] + (2.0 * pushed + wet * (hor_mix * lap - vert_mix * pushed))
    temp1 = base_ref[4:8, :] + wet * (vert_mix * pushed)
    cur0 = base_ref[NSEA : NSEA + 4, :] - wet * (press_grad * (ahead - behind))
    top_ref[...] = jnp.concatenate([temp0, temp1, cur0, jnp.zeros((4, COLS), f32)], axis=0)
    table = jnp.concatenate([temp0, temp0, cur0, cur0], axis=0)
    row = iota((16, COLS), 0)
    aux = aux_ref[...][:, :16]
    for slot in range(2):
        for c in range(2):
            part = jnp.where(row // 4 == 2 * c + slot, table, 0.0).astype(bf16)
            s_ref[pl.ds(2 * slot + c, ntile, stride=4), :] = dot(aux, part, 1, 0)
    sent_ref[...] = s_ref[...].astype(bf16)


def air_kernel(q_ref, c_ref, b_ref, a_ref, fe_ref, fw_ref, base_ref, top_ref, air_ref, sea_ref, fb_s, fo_s, fa_s, b_s, a_s):
    sea_ref[...] = base_ref[...]
    sea_ref[0:8, :] = top_ref[0:8, :]
    sea_ref[NSEA : NSEA + 4, :] = top_ref[8:12, :]
    fb_s[...] = beyond_of(b_ref)
    fo_s[...] = beyond(fe_ref[:, :NOWN], fw_ref[:, :NOWN])
    fa_s[...] = beyond_of(a_ref)
    b_s[...] = b_ref[0:NAIR, :].astype(f32)
    a_s[...] = a_ref[0:NAIR, :].astype(f32)

    def chunk(i, _):
        at = i * 8 * ROWS

        def take(ref, start):
            return ref[pl.ds(start + at, 8, stride=ROWS), :]

        fields = []
        for k in range(3):
            rows = []
            for r in range(ROWS):
                rows.append((take(b_s, k * NA1 + r), take(fb_s, k * NA1 + r)))
            for r in range(ROWS):
                own = take(q_ref, r) if k == 0 else take(c_ref, (k - 1) * NA1 + r)
                rows.append((own, take(fo_s, k * NA1 + r)))
            for r in range(ROWS):
                rows.append((take(a_s, k * NA1 + r), take(fa_s, k * NA1 + r)))
            fields.append([jnp.concatenate(p, axis=1) for p in rows])
        q, cx, cy = fields
        yp, ym = [jnp.maximum(g, 0.0) for g in cy], [jnp.minimum(g, 0.0) for g in cy]
        coefs = [None]
        for j in range(1, 3 * ROWS - 1):
            xp, xm = jnp.maximum(cx[j], 0.0), jnp.minimum(cx[j], 0.0)
            coefs.append((1.0 - xp + pltpu.roll(xm, 1, 1) - yp[j] + ym[j - 1], pltpu.roll(xp, 1, 1), xm))
        for step in range(NSTEP):
            new = []
            for j in range(1, len(q) - 1):
                a0, aw, xm = coefs[step + j]
                west, east = pltpu.roll(q[j], 1, 1), pltpu.roll(q[j], 2 * COLS - 1, 1)
                rest = yp[step + j - 1] * q[j - 1] - ym[step + j] * q[j + 1]
                new.append((a0 * q[j] + aw * west - xm * east) + rest)
            q = new
        for r in range(ROWS):
            air_ref[pl.ds(at + r, 8, stride=ROWS), :] = q[r][:, :COLS]
        return 0

    lax.fori_loop(0, LEV // 8, chunk, 0)


def back_kernel(came_ref, w_ref, want_ref, area_ref, out_ref):
    values = dot(want_ref[...], came_ref[...], 1, 0).astype(bf16)
    pairs = dot(values, w_ref[...], 1, 1)
    e, l = iota((PADE, SUB * ENTS), 0), iota((PADE, SUB * ENTS), 1)
    mine = l // SUB == e
    halves = (pairs[:PADE], pairs[PADE:])
    sums = [jnp.sum(jnp.where(mine, h, 0.0), axis=0, keepdims=True) for h in halves]
    out_ref[...] = line_up(sums) / area_ref[...]


def body(
    atmosphere_tracer_state,
    courant,
    surface_exchange_factor,
    prior_sea_surface_temper,
    remap_overlay_weight,
    remap_dest_tile,
    remap_dest_block,
    ocean_level_state,
    ocean_cell_mask,
):
    ntile = lax.axis_size("tile")
    sds = jax.ShapeDtypeStruct
    q = atmosphere_tracer_state.reshape(NA1, COLS)
    c = courant.reshape(2 * NA1, COLS)
    x = ocean_level_state.reshape(2 * NSEA, COLS)
    mask = ocean_cell_mask
    weights = remap_overlay_weight.reshape(ENTS * SUB, COLS)
    tiles = jnp.pad(remap_dest_tile[0], (0, PADE - ENTS), constant_values=-1000)
    blocks = jnp.pad(remap_dest_block[0], (0, PADE - ENTS))
    tcol, bcol = tiles[:, None], blocks[:, None]
    trow = jnp.tile(tiles, 4)[None, :]

    stay = (lambda a: a) if INTERPRET else (lambda a: pltpu.with_memory_space_constraint(a, pltpu.HBM))
    low, x = call(
        low_kernel, (sds((16, COLS), bf16), sds(x.shape, f32)), stay(q), stay(c), stay(x), far=3,
        scratch=[pltpu.VMEM((24, COLS), f32), pltpu.SemaphoreType.DMA((4,))],
    )
    low_b = lax.ppermute(low, "comp", ring("comp", 1))
    low_a = lax.ppermute(low, "comp", ring("comp", -1))
    strip = sds((8, NSTR), bf16)
    west, east = call(strip_kernel, (strip, strip), q, c, x, mask, low, low_b, low_a)
    slots = sds((4 * ntile, COLS), bf16)
    tcol, west, east = lax.optimization_barrier((tcol, west, east))
    fe = lax.ppermute(west, "tile", ring("tile", -1))
    fw = lax.ppermute(east, "tile", ring("tile", 1))
    spread, masks, want, areas = call(
        functools.partial(table_kernel, ntile),
        (sds((4 * ntile, 4 * PADE), bf16), sds((3 * PADE, COLS), f32), sds((2 * PADE, 4 * ntile), bf16), sds((8, COLS), f32)),
        tcol, trow, bcol, weights,
    )
    outgoing = call(
        flux_kernel, slots,
        q, c, low_b, low_a, fe, fw, surface_exchange_factor, prior_sea_surface_temper, weights, spread, masks,
    )
    outgoing, fe1 = lax.optimization_barrier((outgoing, fe))

    def exchange(a):
        a = a.reshape(ntile, 4, COLS)
        return lax.all_to_all(a, "tile", split_axis=0, concat_axis=0, tiled=True).reshape(4 * ntile, COLS)

    far = [pltpu.VMEM((NOWN, COLS), f32)] * 3
    arrived = exchange(outgoing)
    msg = sds((NMSG, COLS), bf16)
    up, down = call(pack_kernel, (msg, msg), q, c, x, mask, fe1, fw)
    before = lax.ppermute(up, "comp", ring("comp", 1))
    after = lax.ppermute(down, "comp", ring("comp", -1))
    base, wide_wet = call(
        sea_kernel, (sds((2 * NSEA, COLS), f32), sds((8, 2 * COLS), f32)),
        x, mask, before, after, fe1, fw, scratch=[pltpu.VMEM((2 * NSEA + 16, COLS), f32)] + far,
    )
    tile8 = sds((8, COLS), f32)
    aux, keep, to_up, to_down = call(
        functools.partial(force_kernel, ntile), (sds((ntile, COLS), bf16), sds((16, COLS), f32), tile8, tile8),
        arrived, wide_wet, scratch=[pltpu.VMEM((4 * ntile, COLS), f32)],
    )
    below = lax.ppermute(to_up, "comp", ring("comp", 1))
    above = lax.ppermute(to_down, "comp", ring("comp", -1))
    sent, top = call(
        functools.partial(surface_kernel, ntile), (slots, sds((16, COLS), f32)),
        base, keep, below, above, aux, scratch=[pltpu.VMEM((4 * ntile, COLS), f32)],
    )
    sent, top = lax.optimization_barrier((sent, top))
    came = exchange(sent)
    air_new, ocean_new = call(
        air_kernel, (sds((NA1, COLS), f32), sds((2 * NSEA, COLS), f32)),
        q, c, before, after, fe, fw, base, top, scratch=far + [pltpu.VMEM((NAIR, COLS), f32)] * 2,
    )
    surface_air = call(back_kernel, tile8, came, weights, want, areas)
    return (
        air_new.reshape(atmosphere_tracer_state.shape),
        ocean_new.reshape(ocean_level_state.shape),
        surface_air.reshape(2, ROWS, COLS),
    )


def solution(mesh):
    return jax.shard_map(
        body,
        mesh=mesh,
        in_specs=(
            P(None, "comp", "tile"),
            P(None, None, "comp", "tile"),
            P("comp", "tile"),
            P("comp", "tile"),
            P("comp", "tile", None, None),
            P("comp", "tile"),
            P("comp", "tile"),
            P(None, None, "comp", "tile"),
            P("comp", "tile"),
        ),
        out_specs=(P(None, "comp", "tile"), P(None, None, "comp", "tile"), P(None, "comp", "tile")),
        check_vma=False,
    )
```
